32 devices in a mesh: ctx: 8 (over z, core), fsdp: 4 (over y, x).
Axes of the slice: x: 2, y: 2, z: 4, core: 2. Of those that a mesh axis runs over, the one named last changes fastest.
Arguments:
- tokens: bfloat16 [4, 4096, 1280], P('fsdp', 'ctx'), may hold values from -6 to 6
- lengths: int32 [4], P('fsdp'), may hold values from 1024 to 4096, as said below
- cotangent: bfloat16 [4, 4096, 1280], P('fsdp', 'ctx'), may hold values from -6 to 6
- gain_one: bfloat16 [1280], P('fsdp'), may hold values from 0.5 to 1.5
- query_weight: bfloat16 [1280, 1280], P('fsdp'), may hold values from -0.15625 to 0.15625
- key_matrix: bfloat16 [1280, 320], P('fsdp'), may hold values from -0.15625 to 0.15625
- value_matrix: bfloat16 [1280, 320], P('fsdp'), may hold values from -0.15625 to 0.15625
- out_weight: bfloat16 [1280, 1280], P('fsdp'), may hold values from -4 to 4
- gain_two: bfloat16 [1280], P('fsdp'), may hold values from 0.5 to 1.5
- gate_weight: bfloat16 [1280, 3584], P('fsdp'), may hold values from -0.15625 to 0.15625
- up_weight: bfloat16 [1280, 3584], P('fsdp'), may hold values from -0.15625 to 0.15625
- down_weight: bfloat16 [3584, 1280], P('fsdp'), may hold values from -0.09375 to 0.09375
Outputs:
- output: bfloat16 [4, 4096, 1280], P('fsdp', 'ctx')
- grad_tokens: bfloat16 [4, 4096, 1280], P('fsdp', 'ctx')
- grad_gain_one: float32 [1280], P('fsdp')
- grad_query: float32 [1280, 1280], P('fsdp')
- grad_key: float32 [1280, 320], P('fsdp')
- grad_value: float32 [1280, 320], P('fsdp')
- grad_out: float32 [1280, 1280], P('fsdp')
- grad_gain_two: float32 [1280], P('fsdp')
- grad_gate: float32 [1280, 3584], P('fsdp')
- grad_up: float32 [1280, 3584], P('fsdp')
- grad_down: float32 [3584, 1280], P('fsdp')
The draws below stay inside these ranges and needn't reach their ends.
Inputs may be any that keep to these rules, and one draw needn't show every extreme that they name: Slot s holds valid tokens at its first lengths[s] positions. One slot of all, chosen by the seed, has length 4096.
All inputs are finite; a program needn't handle non-finite values.
Results may differ from the reference program's by a relative error of at most 0.024.
Values may be sent and summed in bfloat16 or wider, within the bound.
No kernel may reach another device: no remote copies, remote signals or barrier semaphores. Data moves between devices by JAX's collectives and lax.ppermute only.
A program may use at most 192 MiB of HBM per device.

```python
import math
import jax
import jax.numpy as jnp
from jax import lax

MODEL_DIM = 1280
QUERY_HEADS = 20
KEY_VALUE_HEADS = 5
HEAD_SIZE = 64
FF = 3584
SLOT_TOKENS = 4096
SLOTS = 4


def draw_lengths(key, part):
    key_drawn = jax.random.fold_in(key, 11)
    key_chosen = jax.random.fold_in(key, 12)
    drawn = jax.random.randint(key_drawn, (SLOTS,), SLOT_TOKENS // 4, SLOT_TOKENS + 1)
    chosen = jax.random.randint(key_chosen, (), 0, SLOTS)
    index_all = jnp.arange(SLOTS)
    return jnp.where(index_all == chosen, SLOT_TOKENS, drawn).astype(jnp.int32)


def levels(stream_key, shape, cuts, least, top_value):
    loudness, own = 1.0, jax.random.fold_in(stream_key, 6)
    for axis_at, shards_of in cuts:
        draws = jnp.exp(jax.random.uniform(jax.random.fold_in(own, axis_at), (shards_of,), jnp.float32, least / len(cuts), top_value / len(cuts)))
        loudness = loudness * jnp.repeat(draws, shape[axis_at] // shards_of).reshape([-1 if axis == axis_at else 1 for axis in range(len(shape))])
    return loudness


def centred(rng, extent, width, most, cuts=(), held_as=jnp.bfloat16):
    entries = jax.random.normal(rng, extent, jnp.float32) * width
    if len(cuts) > 0:
        entries = levels(rng, extent, cuts, -0.22, 0.18) * entries
    return jnp.clip(entries, min=-most, max=most).astype(held_as)


def setup_inputs(seed: int = 0) -> dict:
    key_list = jax.random.split(jax.random.key(seed), 13)
    tokens = centred(key_list[0], (SLOTS, SLOT_TOKENS, MODEL_DIM), 1.0, 6.0, ((0, 4), (1, 8)))
    lengths = draw_lengths(jax.random.fold_in(key_list[12], 71), 0)
    cotangent = centred(key_list[2], (SLOTS, SLOT_TOKENS, MODEL_DIM), 1.0, 6.0, ((0, 4), (1, 8)))
    gain_one = jnp.clip(1.0 + 0.1 * jax.random.normal(key_list[3], (MODEL_DIM,), jnp.float32), 0.5, 1.5).astype(jnp.bfloat16)
    query_weight = centred(key_list[4], (MODEL_DIM, QUERY_HEADS * HEAD_SIZE), MODEL_DIM ** -0.5, 0.15625, ((0, 4),))
    key_matrix = centred(key_list[5], (MODEL_DIM, KEY_VALUE_HEADS * HEAD_SIZE), MODEL_DIM ** -0.5, 0.15625, ((0, 4),))
    value_matrix = centred(key_list[6], (MODEL_DIM, KEY_VALUE_HEADS * HEAD_SIZE), MODEL_DIM ** -0.5, 0.15625, ((0, 4),))
    out_weight = centred(key_list[7], (QUERY_HEADS * HEAD_SIZE, MODEL_DIM), (QUERY_HEADS * HEAD_SIZE * 8 // SLOT_TOKENS) ** -0.5, 4.0, ((0, 4),))
    gain_two = jnp.clip(1.0 + 0.1 * jax.random.normal(key_list[8], (MODEL_DIM,), jnp.float32), 0.5, 1.5).astype(jnp.bfloat16)
    gate_weight = centred(key_list[9], (MODEL_DIM, FF), MODEL_DIM ** -0.5, 0.15625, ((0, 4),))
    up_weight = centred(key_list[10], (MODEL_DIM, FF), MODEL_DIM ** -0.5, 0.15625, ((0, 4),))
    down_weight = centred(key_list[11], (FF, MODEL_DIM), FF ** -0.5, 0.09375, ((0, 4),))
    return dict(tokens=tokens, lengths=lengths, cotangent=cotangent, gain_one=gain_one, query_weight=query_weight, key_matrix=key_matrix, value_matrix=value_matrix, out_weight=out_weight, gain_two=gain_two, gate_weight=gate_weight, up_weight=up_weight, down_weight=down_weight)


@jax.custom_vjp
def lower_precision(v):
    return lax.optimization_barrier(v.astype(jnp.bfloat16)).astype(jnp.float32)

@jax.custom_vjp
def lower_backward(v):
    return v

def low_keep(v):
    return (lower_precision(v), None)

def low_pass(kept, grad):
    return (grad,)

def back_keep(v):
    return (v, None)

def back_low(kept, grad):
    return (lower_precision(grad),)
lower_precision.defvjp(low_keep, low_pass)
lower_backward.defvjp(back_keep, back_low)
highest = lax.Precision.HIGHEST
epsilon = 1e-05

def matrix_product(left_side, right_side):
    return jnp.dot(left_side, right_side, precision=highest)

def apply_rotation(vectors, cosine_factor, sine_factor):
    half_size = vectors.shape[-1] // 2
    first_half = vectors[..., :half_size]
    second_half = vectors[..., half_size:]
    return jnp.concatenate([first_half * cosine_factor - second_half * sine_factor, second_half * cosine_factor + first_half * sine_factor], -1)

def angles(positions):
    exponent = jnp.arange(HEAD_SIZE // 2).astype(jnp.float32) * (2.0 / HEAD_SIZE)
    frequency = jnp.power(10000.0, -exponent)
    phase_angle = positions.astype(jnp.float32)[:, None] * frequency[None, :]
    return (jnp.cos(phase_angle)[:, None, :], jnp.sin(phase_angle)[:, None, :])

def rms_scale(values):
    return lax.rsqrt(lax.optimization_barrier(jnp.mean(values * values, -1, keepdims=True)) + epsilon)

def slot_forward(params, tokens, length):
    gain_one, query_weight, key_matrix, value_matrix, out_weight, gain_two, gate_weight, up_weight, down_weight = params
    positions = jnp.arange(SLOT_TOKENS)
    cosine_factor, sine_factor = angles(positions)
    normalized_input = lower_precision(tokens * rms_scale(tokens) * gain_one)
    query_rows = lower_precision(apply_rotation(lower_backward(matrix_product(normalized_input, query_weight)).reshape(SLOT_TOKENS, QUERY_HEADS, HEAD_SIZE), cosine_factor, sine_factor))
    key_row_block = lower_precision(apply_rotation(lower_backward(matrix_product(normalized_input, key_matrix)).reshape(SLOT_TOKENS, KEY_VALUE_HEADS, HEAD_SIZE), cosine_factor, sine_factor))
    value_row_block = lower_precision(lower_backward(matrix_product(normalized_input, value_matrix))).reshape(SLOT_TOKENS, KEY_VALUE_HEADS, HEAD_SIZE)
    key_valid = positions < length
    row_block_size = min(512, SLOT_TOKENS)
    score_scale = 1.0 / math.sqrt(HEAD_SIZE)

    def attend(block_item):
        query_block, query_pos = block_item
        scores = lower_backward(score_scale * jnp.einsum('qhgd,khd->hgqk', query_block, key_row_block, precision=highest))
        allowed = (positions[None, :] <= query_pos[:, None]) & key_valid[None, :]
        scores = jnp.where(allowed[None, None], scores, -1e+30)
        shifted = jnp.exp(scores - lax.optimization_barrier(jnp.max(scores, -1, keepdims=True)))
        weights = lower_precision(shifted / lax.optimization_barrier(jnp.sum(shifted, -1, keepdims=True)))
        return jnp.einsum('hgqk,khd->qhgd', weights, value_row_block, precision=highest)
    grouped_heads = query_rows.reshape(SLOT_TOKENS // row_block_size, row_block_size, KEY_VALUE_HEADS, QUERY_HEADS // KEY_VALUE_HEADS, HEAD_SIZE)
    attended = lax.map(jax.checkpoint(attend), (grouped_heads, positions.reshape(SLOT_TOKENS // row_block_size, row_block_size)))
    attended = lower_precision(lower_backward(attended.reshape(SLOT_TOKENS, QUERY_HEADS * HEAD_SIZE)))
    hidden = tokens + lower_backward(matrix_product(attended, out_weight))
    normed_two = lower_precision(hidden * rms_scale(hidden) * gain_two)
    gate_pre = lower_backward(matrix_product(normed_two, gate_weight))
    up_pre = lower_backward(matrix_product(normed_two, up_weight))
    inner_act = lower_precision(jax.nn.silu(gate_pre) * up_pre)
    result = hidden + lower_backward(matrix_product(inner_act, down_weight))
    valid_rows = (positions < length).astype(jnp.float32)[:, None]
    return valid_rows * result

def reference(tokens, lengths, cotangent, gain_one, query_weight, key_matrix, value_matrix, out_weight, gain_two, gate_weight, up_weight, down_weight):
    params = tuple((weight.astype(jnp.float32) for weight in (gain_one, query_weight, key_matrix, value_matrix, out_weight, gain_two, gate_weight, up_weight, down_weight)))

    def one_slot(totals, slot_item):
        slot_tokens, length, slot_cot = slot_item

        def forward(weights_all, token_rows):
            return slot_forward(weights_all, token_rows, length)
        result, pull_back = jax.vjp(forward, params, slot_tokens.astype(jnp.float32))
        weight_grads, token_grads = pull_back(slot_cot.astype(jnp.float32))
        totals = tuple((running + grad_part for running, grad_part in zip(totals, weight_grads)))
        return (totals, (result.astype(jnp.bfloat16), token_grads.astype(jnp.bfloat16)))
    zeros_init = tuple((jnp.zeros_like(weight) for weight in params))
    totals, outputs = lax.scan(one_slot, zeros_init, (tokens, lengths, cotangent))
    return (outputs[0], outputs[1], totals[0], totals[1], totals[2], totals[3], totals[4], totals[5], totals[6], totals[7], totals[8])
```

```python
import functools
import math

import jax
import jax.numpy as jnp
from jax import lax
from jax.experimental import pallas as pl
from jax.experimental.pallas import tpu as pltpu
from jax.sharding import PartitionSpec as P

QUERY_HEADS = 20
KEY_VALUE_HEADS = 5
GROUP = QUERY_HEADS // KEY_VALUE_HEADS
HEAD_SIZE = 64
PAIR = 2 * HEAD_SIZE
HALF_HEAD = HEAD_SIZE // 2
epsilon = 1e-05
LOG2E = math.log2(math.e)
SCORE_SCALE = 1.0 / math.sqrt(HEAD_SIZE)
NEGATIVE = -1e30
EXTRA = 16
f32 = jnp.float32
bf16 = jnp.bfloat16


def rms_scale(values):
    return lax.rsqrt(jnp.mean(values * values, -1, keepdims=True) + epsilon)


def norm_back(grad_normed, values, scale_rows, gain):
    weighted = grad_normed * gain
    cubed = scale_rows * scale_rows * scale_rows
    return scale_rows * weighted - values * cubed * jnp.mean(weighted * values, -1, keepdims=True)


def swap_halves(x):
    lane = lax.broadcasted_iota(jnp.int32, x.shape, 1)
    ahead = pltpu.roll(x, PAIR - HALF_HEAD, 1)
    behind = pltpu.roll(x, HALF_HEAD, 1)
    return jnp.where(lane % HEAD_SIZE < HALF_HEAD, ahead, behind)


def project_kernel(x_ref, w_ref, cos_ref, sin_ref, q_ref, kv_ref):
    step = pl.program_id(0)
    width = w_ref.shape[1]
    product = jnp.dot(x_ref[...], w_ref[...], preferred_element_type=f32)
    is_pair = step == pl.num_programs(0) - 1
    lane = lax.broadcasted_iota(jnp.int32, cos_ref.shape, 1)
    plain = jnp.logical_and(is_pair, lane >= HEAD_SIZE)
    cos = jnp.where(plain, 1.0, cos_ref[...])
    sin = jnp.where(plain, 0.0, sin_ref[...])
    pieces = []
    for at in range(0, width, PAIR):
        part = product[:, at : at + PAIR]
        pieces.append((part * cos + swap_halves(part) * sin).astype(bf16))

    @pl.when(is_pair)
    def _():
        for i, piece in enumerate(pieces):
            kv_ref[:, i * PAIR : (i + 1) * PAIR] = piece

    @pl.when(jnp.logical_not(is_pair))
    def _():
        for i, piece in enumerate(pieces):
            q_ref[:, i * PAIR : (i + 1) * PAIR] = piece


def project(normed, weights, cos, sin):
    rows, model = normed.shape
    width = KEY_VALUE_HEADS * PAIR
    steps = weights.shape[1] // width
    return pl.pallas_call(
        project_kernel,
        grid=(steps,),
        in_specs=[
            pl.BlockSpec((rows, model), lambda i: (0, 0)),
            pl.BlockSpec((model, width), lambda i: (0, i)),
            pl.BlockSpec((rows, PAIR), lambda i: (0, 0)),
            pl.BlockSpec((rows, PAIR), lambda i: (0, 0)),
        ],
        out_specs=[
            pl.BlockSpec((rows, width), lambda i: (0, jnp.minimum(i, steps - 2))),
            pl.BlockSpec((rows, width), lambda i: (0, 0)),
        ],
        out_shape=[
            jax.ShapeDtypeStruct((rows, width * (steps - 1)), bf16),
            jax.ShapeDtypeStruct((rows, width), bf16),
        ],
        compiler_params=pltpu.CompilerParams(vmem_limit_bytes=40 << 20),
        cost_estimate=pl.CostEstimate(
            flops=2 * rows * model * width * steps,
            bytes_accessed=2 * model * width * steps + 4 * rows * model,
            transcendentals=0,
        ),
        name="project",
    )(normed, weights, cos, sin)


def unrotate_kernel(x_ref, cos_ref, sin_ref, out_ref):
    lane = lax.broadcasted_iota(jnp.int32, cos_ref.shape, 1)
    cos = jnp.where(lane >= HEAD_SIZE, 1.0, cos_ref[...])
    sin = jnp.where(lane >= HEAD_SIZE, 0.0, sin_ref[...])
    for at in range(0, x_ref.shape[1], PAIR):
        part = x_ref[:, at : at + PAIR].astype(f32)
        out_ref[:, at : at + PAIR] = (part * cos - swap_halves(part) * sin).astype(bf16)


def unrotate(x, cos, sin):
    return pl.pallas_call(
        unrotate_kernel, out_shape=jax.ShapeDtypeStruct(x.shape, bf16), name="unrotate"
    )(x, cos, sin)


def block_row(block, blocks, half):
    device = jnp.minimum(block, blocks - 1 - block)
    return pl.multiple_of(device * (2 * half) + (block % 2) * half, half)


def two_blocks(ref, step, blocks, half):
    first = ref[pl.ds(block_row(2 * step, blocks, half), half), :]
    second = ref[pl.ds(block_row(2 * step + 1, blocks, half), half), :]
    return jnp.concatenate([first, second], 0)


def one_head(ref, rows, head, low):
    part = ref[rows, (head // 2) * PAIR : (head // 2 + 1) * PAIR].astype(f32)
    lane = lax.broadcasted_iota(jnp.int32, part.shape, 1)
    if (head % 2 == 0) != low:
        part = pltpu.roll(part, HEAD_SIZE, 1)
    keep = lane < HEAD_SIZE if low else lane >= HEAD_SIZE
    return jnp.where(keep, part, 0.0).astype(bf16)


def allowed_keys(step, block, length, half):
    shape = (2 * half, half)
    key_pos = lax.broadcasted_iota(jnp.int32, shape, 0) + step * (2 * half)
    query_pos = lax.broadcasted_iota(jnp.int32, shape, 1) + block * half
    return key_pos <= jnp.minimum(query_pos, length - 1)


def key_steps(block, length, half):
    keys = jnp.minimum((block + 1) * half, length)
    return (keys + 2 * half - 1) // (2 * half)


LAST = (((1,), (1,)), ((), ()))


def forward_kernel(blocks, info_ref, q_ref, kv_ref, o_ref, lse_ref, q_sc, m_sc, l_sc, acc_sc):
    half = q_ref.shape[0] // 2
    length = info_ref[0]
    for slot in range(2):
        block = info_ref[1 + slot]
        rows = slice(slot * half, (slot + 1) * half)
        for head in range(GROUP):
            q_sc[head] = one_head(q_ref, rows, head, True)
        m_sc[...] = jnp.full_like(m_sc, NEGATIVE)
        l_sc[...] = jnp.zeros_like(l_sc)
        acc_sc[...] = jnp.zeros_like(acc_sc)

        def work(step, masked):
            pair = two_blocks(kv_ref, step, blocks, half)
            pair_t = pair.T
            if masked:
                allowed = allowed_keys(step, block, length, half)
            for head in range(GROUP):
                scores = lax.dot_general(pair, q_sc[head], LAST, preferred_element_type=f32)
                scores = scores * (SCORE_SCALE * LOG2E)
                if masked:
                    scores = jnp.where(allowed, scores, NEGATIVE)
                m_old = m_sc[head]
                m_new = jnp.maximum(m_old, jnp.max(scores, 0, keepdims=True))
                weights = jnp.exp2(scores - m_new)
                fading = jnp.exp2(m_old - m_new)
                m_sc[head] = m_new
                l_sc[head] = l_sc[head] * fading + jnp.sum(weights, 0, keepdims=True)
                acc_sc[head] = acc_sc[head] * fading + jnp.dot(
                    pair_t, weights.astype(bf16), preferred_element_type=f32
                )

        steps = key_steps(block, length, half)

        @pl.loop(0, steps - 1)
        def _(step):
            work(step, False)

        work(steps - 1, True)
        for at in range(0, GROUP, 2):
            two = [
                acc_sc[head][HEAD_SIZE:, :] / l_sc[head] for head in (at, at + 1)
            ]
            o_ref[rows, at * HEAD_SIZE : (at + 2) * HEAD_SIZE] = (
                jnp.concatenate(two, 0).T.astype(bf16)
            )
        for head in range(GROUP):
            lse_ref[0, head : head + 1, rows] = m_sc[head] + jnp.log2(l_sc[head])


def attend(q, pairs, info):
    rows, keys = q.shape[0], pairs.shape[0]
    half = rows // 2
    width = GROUP * HEAD_SIZE
    work = QUERY_HEADS * rows * (keys // 2)
    return pl.pallas_call(
        functools.partial(forward_kernel, keys // half),
        grid_spec=pltpu.PrefetchScalarGridSpec(
            num_scalar_prefetch=1,
            grid=(KEY_VALUE_HEADS,),
            in_specs=[
                pl.BlockSpec((rows, width), lambda g, info: (0, g)),
                pl.BlockSpec((keys, PAIR), lambda g, info: (0, g)),
            ],
            out_specs=[
                pl.BlockSpec((rows, width), lambda g, info: (0, g)),
                pl.BlockSpec((1, GROUP, rows), lambda g, info: (g, 0, 0)),
            ],
            scratch_shapes=[
                pltpu.VMEM((GROUP, half, PAIR), bf16),
                pltpu.VMEM((GROUP, 1, half), f32),
                pltpu.VMEM((GROUP, 1, half), f32),
                pltpu.VMEM((GROUP, PAIR, half), f32),
            ],
        ),
        out_shape=[
            jax.ShapeDtypeStruct(q.shape, bf16),
            jax.ShapeDtypeStruct((KEY_VALUE_HEADS, GROUP, rows), f32),
        ],
        compiler_params=pltpu.CompilerParams(vmem_limit_bytes=40 << 20),
        cost_estimate=pl.CostEstimate(
            flops=16 * work * HEAD_SIZE, bytes_accessed=2 * keys * 640, transcendentals=work
        ),
        name="attend",
    )(info, q, pairs)


def backward_kernel(
    blocks, info_ref, q_ref, do_ref, o_ref, lse_ref, kv_ref, cos_ref, sin_ref,
    dq_ref, dkv_ref, both_sc, delta_sc, dq_sc, dkv_sc, terms_sc,
):
    half = q_ref.shape[0] // 2
    length = info_ref[0]
    dkv_sc[...] = jnp.zeros_like(dkv_sc)
    for slot in range(2):
        block = info_ref[1 + slot]
        rows = slice(slot * half, (slot + 1) * half)
        for head in range(GROUP):
            both_sc[2 * head] = one_head(q_ref, rows, head, True)
            both_sc[2 * head + 1] = one_head(do_ref, rows, head, False)
        for at in range(0, GROUP, 2):
            lanes = slice(at * HEAD_SIZE, (at + 2) * HEAD_SIZE)
            product = (do_ref[rows, lanes].astype(f32) * o_ref[rows, lanes].astype(f32)).T
            for i in range(2):
                delta_sc[at + i] = jnp.sum(
                    product[i * HEAD_SIZE : (i + 1) * HEAD_SIZE], 0, keepdims=True
                )
        dq_sc[...] = jnp.zeros_like(dq_sc)

        def work(step, masked):
            pair = two_blocks(kv_ref, step, blocks, half)
            pair_t = pair.T
            if masked:
                allowed = allowed_keys(step, block, length, half)
            for head in range(GROUP):
                scores = lax.dot_general(pair, both_sc[2 * head], LAST, preferred_element_type=f32)
                lse = lse_ref[0, head : head + 1, rows]
                probs = jnp.exp2(scores * (SCORE_SCALE * LOG2E) - lse)
                if masked:
                    probs = jnp.where(allowed, probs, 0.0)
                grad_probs = lax.dot_general(
                    pair, both_sc[2 * head + 1], LAST, preferred_element_type=f32
                )
                grad_scores = (probs * (grad_probs - delta_sc[head])).astype(bf16)
                terms_sc[:, 2 * head * half : (2 * head + 1) * half] = grad_scores
                terms_sc[:, (2 * head + 1) * half : (2 * head + 2) * half] = probs.astype(bf16)
                dq_sc[head] += jnp.dot(pair_t, grad_scores, preferred_element_type=f32)
            update = jnp.dot(
                terms_sc[...],
                both_sc[...].reshape(2 * GROUP * half, PAIR),
                preferred_element_type=f32,
            )
            for i in range(2):
                at = pl.ds(block_row(2 * step + i, blocks, half), half)
                dkv_sc[at, :] += update[i * half : (i + 1) * half]

        steps = key_steps(block, length, half)

        @pl.loop(0, steps - 1)
        def _(step):
            work(step, False)

        work(steps - 1, True)
        for at in range(0, GROUP, 2):
            two = [dq_sc[head][:HEAD_SIZE, :] for head in (at, at + 1)]
            grad = jnp.concatenate(two, 0).T * SCORE_SCALE
            grad = grad * cos_ref[rows, :] - swap_halves(grad) * sin_ref[rows, :]
            dq_ref[rows, at * HEAD_SIZE : (at + 2) * HEAD_SIZE] = grad.astype(bf16)
    lane = lax.broadcasted_iota(jnp.int32, dkv_sc.shape, 1)
    dkv_ref[...] = jnp.where(lane < HEAD_SIZE, dkv_sc[...] * SCORE_SCALE, dkv_sc[...]).astype(bf16)


def attend_back(q, grad, attended, lse, pairs, cos, sin, info):
    rows, keys = q.shape[0], pairs.shape[0]
    half = rows // 2
    width = GROUP * HEAD_SIZE
    work = QUERY_HEADS * rows * (keys // 2)
    head_block = pl.BlockSpec((rows, width), lambda g, info: (0, g))
    key_block = pl.BlockSpec((keys, PAIR), lambda g, info: (0, g))
    table = pl.BlockSpec((rows, PAIR), lambda g, info: (0, 0))
    return pl.pallas_call(
        functools.partial(backward_kernel, keys // half),
        grid_spec=pltpu.PrefetchScalarGridSpec(
            num_scalar_prefetch=1,
            grid=(KEY_VALUE_HEADS,),
            in_specs=[
                head_block,
                head_block,
                head_block,
                pl.BlockSpec((1, GROUP, rows), lambda g, info: (g, 0, 0)),
                key_block,
                table,
                table,
            ],
            out_specs=[head_block, key_block],
            scratch_shapes=[
                pltpu.VMEM((2 * GROUP, half, PAIR), bf16),
                pltpu.VMEM((GROUP, 1, half), f32),
                pltpu.VMEM((GROUP, PAIR, half), f32),
                pltpu.VMEM((keys, PAIR), f32),
                pltpu.VMEM((2 * half, 2 * GROUP * half), bf16),
            ],
        ),
        out_shape=[
            jax.ShapeDtypeStruct(q.shape, bf16),
            jax.ShapeDtypeStruct(pairs.shape, bf16),
        ],
        compiler_params=pltpu.CompilerParams(vmem_limit_bytes=48 << 20),
        cost_estimate=pl.CostEstimate(
            flops=40 * work * HEAD_SIZE, bytes_accessed=8 * keys * 640, transcendentals=work
        ),
        name="attend_back",
    )(info, q, grad, attended, lse, pairs, cos, sin)


def place_kernel(count, spots_ref, *refs):
    out_ref, sems = refs[count], refs[count + 1]
    copies = []
    for i, ref in enumerate(refs[:count]):
        start = pl.multiple_of(spots_ref[i], 16)
        copy = pltpu.make_async_copy(ref, out_ref.at[pl.ds(start, ref.shape[0])], sems.at[i])
        copy.start()
        copies.append(copy)
    for copy in copies:
        copy.wait()


def place(pieces, spots, rows):
    count = len(pieces)
    anywhere = pl.BlockSpec(memory_space=pl.ANY)
    width = pieces[0].shape[1]
    return pl.pallas_call(
        functools.partial(place_kernel, count),
        grid_spec=pltpu.PrefetchScalarGridSpec(
            num_scalar_prefetch=1,
            grid=(1,),
            in_specs=[anywhere] * count,
            out_specs=pl.BlockSpec((rows, width), lambda i, spots: (0, 0)),
            scratch_shapes=[pltpu.SemaphoreType.DMA((count,))],
        ),
        out_shape=jax.ShapeDtypeStruct((rows, width), pieces[0].dtype),
        compiler_params=pltpu.CompilerParams(vmem_limit_bytes=24 << 20),
        cost_estimate=pl.CostEstimate(
            flops=0, bytes_accessed=4 * rows * width, transcendentals=0
        ),
        name="place",
    )(jnp.stack(spots).astype(jnp.int32), *pieces)


def split_kernel(parts, core_ref, gate_ref, up_ref, out_ref):
    width = gate_ref.shape[1] // parts // 2
    for core in range(2):

        @pl.when(core_ref[0] == core)
        def _():
            taken = []
            for ref in (gate_ref, up_ref):
                for i in range(parts):
                    at = (2 * i + core) * width
                    taken.append(ref[:, at : at + width])
            out_ref[...] = jnp.concatenate(taken, 1)


def split_columns(core, gate, up, parts):
    rows, width = gate.shape
    block = rows // 2
    spec = pl.BlockSpec((block, width), lambda i, core: (i, 0))
    return pl.pallas_call(
        functools.partial(split_kernel, parts),
        grid_spec=pltpu.PrefetchScalarGridSpec(
            num_scalar_prefetch=1, grid=(2,), in_specs=[spec, spec], out_specs=spec
        ),
        out_shape=jax.ShapeDtypeStruct((rows, width), gate.dtype),
        cost_estimate=pl.CostEstimate(
            flops=0, bytes_accessed=6 * rows * width, transcendentals=0
        ),
        name="split_columns",
    )(core, gate, up)


def merge_kernel(parts, core_ref, own_ref, other_ref, gate_ref, up_ref):
    width = gate_ref.shape[1] // parts // 2
    for core in range(2):

        @pl.when(core_ref[0] == core)
        def _():
            by_core = (own_ref, other_ref) if core == 0 else (other_ref, own_ref)
            for n, out_ref in enumerate((gate_ref, up_ref)):
                taken = []
                for i in range(parts):
                    at = (n * parts + i) * width
                    for ref in by_core:
                        taken.append(ref[:, at : at + width].astype(f32))
                out_ref[...] = jnp.concatenate(taken, 1)


def merge_columns(core, own, other, parts):
    rows, width = own.shape
    block = rows // 4 if rows % 64 == 0 else rows // 2
    spec = pl.BlockSpec((block, width), lambda i, core: (i, 0))
    out = jax.ShapeDtypeStruct((rows, width), f32)
    return pl.pallas_call(
        functools.partial(merge_kernel, parts),
        grid_spec=pltpu.PrefetchScalarGridSpec(
            num_scalar_prefetch=1,
            grid=(rows // block,),
            in_specs=[spec, spec],
            out_specs=[spec, spec],
        ),
        out_shape=[out, out],
        compiler_params=pltpu.CompilerParams(vmem_limit_bytes=24 << 20),
        cost_estimate=pl.CostEstimate(
            flops=0, bytes_accessed=12 * rows * width, transcendentals=0
        ),
        name="merge_columns",
    )(core, own, other)


def after(value, *others):
    return lax.optimization_barrier((value,) + others)[0]


class Moves:
    def __init__(self):
        self.ctx, self.fsdp = lax.axis_size("ctx"), lax.axis_size("fsdp")
        self.me, self.where = lax.axis_index("fsdp"), lax.axis_index("ctx")
        self.core = self.where % 2
        self.square = self.fsdp == 4
        self.line = self.ctx == 8

    def across(self, value, bit):
        return lax.ppermute(value, "fsdp", [(i, i ^ bit) for i in range(self.fsdp)])

    def swap(self, value):
        return lax.ppermute(value, "ctx", [(i, i ^ 1) for i in range(self.ctx)])

    def pick(self, low, high):
        return jnp.where(self.core == 0, low, high)

    def owner(self, half):
        return half if half < self.ctx else 2 * self.ctx - 1 - half

    def balance(self, rows):
        half = rows.shape[0] // 2
        return jnp.concatenate(
            [
                lax.ppermute(
                    rows[i * half : (i + 1) * half],
                    "ctx",
                    [(d, self.owner(2 * d + i)) for d in range(self.ctx)],
                )
                for i in range(2)
            ],
            0,
        )

    def restore(self, rows):
        half = rows.shape[0] // 2
        return jnp.concatenate(
            [
                lax.ppermute(
                    rows[i * half : (i + 1) * half],
                    "ctx",
                    [(self.owner(2 * d + i), d) for d in range(self.ctx)],
                )
                for i in range(2)
            ],
            0,
        )

    def gather(self, own, gate=None):
        if not self.square:
            whole = lax.all_gather(own, "fsdp", axis=0, tiled=True)
            return whole, None
        if gate is not None:
            own = after(own, *gate)
        rows = own.shape[0]
        half = rows // 32 * 16
        by_x, by_y = self.across(own, 1), self.across(own, 2)
        top, bottom = self.across(by_x[:half], 2), self.across(by_y[half:], 1)
        me = self.me
        spots = [me * rows, (me ^ 1) * rows, (me ^ 2) * rows, (me ^ 3) * rows, (me ^ 3) * rows + half]
        whole = place([own, by_x, by_y, top, bottom], spots, 4 * rows)
        return whole, (by_x, by_y)

    def scatter(self, whole):
        if not self.square:
            rows = whole.shape[1]
            return lax.psum_scatter(
                whole.reshape(self.fsdp * rows, -1), "fsdp", scatter_dimension=0, tiled=True
            )
        part = lambda bit: lax.dynamic_index_in_dim(whole, self.me ^ bit, 0, keepdims=False)
        rows = whole.shape[1]
        half = rows // 32 * 16
        far = part(3)
        top, bottom = self.across(far[:half], 1), self.across(far[half:], 2)
        near_x, near_y = part(1), part(2)
        to_x = jnp.concatenate([near_x[:half], near_x[half:] + bottom], 0)
        to_y = jnp.concatenate([near_y[:half] + top, near_y[half:]], 0)
        return part(0) + self.across(to_x, 1) + self.across(to_y, 2)

    def total(self, part):
        if not self.line:
            groups = [list(range(c, self.ctx, 2)) for c in range(2)]
            return lax.psum(part, "ctx", axis_index_groups=groups)
        move = lambda value, pairs: lax.ppermute(
            value, "ctx", [(2 * a + c, 2 * b + c) for a, b in pairs for c in range(2)]
        )
        inner = part + move(part, [(0, 1), (3, 2)])
        summed = lax.optimization_barrier(inner + move(inner, [(1, 2), (2, 1)]))
        outer = move(summed, [(1, 0), (2, 3)])
        z = self.where // 2
        return jnp.where((z == 0) | (z == 3), outer, summed)

    def both_cores(self, part):
        other = self.swap(part)
        return self.pick(part, other), self.pick(other, part)

    def gather_rows(self, own, gate=None):
        rows, width = own.shape
        half = rows // 2
        mine = self.pick(own[:half], own[half:])
        whole, token = self.gather(mine, gate)
        low, high = self.both_cores(whole)
        shape = (self.fsdp, half, width)
        full = jnp.stack([low.reshape(shape), high.reshape(shape)], 1)
        return full.reshape(self.fsdp * rows, width), token

    def reduce_rows(self, grad, extra=None):
        rows = grad.shape[0] // self.fsdp
        parts = grad.reshape(self.fsdp, 2, rows // 2, grad.shape[1])
        if extra is not None:
            parts = jnp.concatenate([parts, extra], 2)
        send = lax.dynamic_index_in_dim(parts, 1 - self.core, 1, keepdims=False)
        keep = lax.dynamic_index_in_dim(parts, self.core, 1, keepdims=False)
        part = self.total(self.scatter(keep + self.swap(send)))
        return self.both_cores(part)


def local(
    tokens,
    lengths,
    cotangent,
    gain_one,
    query_weight,
    key_matrix,
    value_matrix,
    out_weight,
    gain_two,
    gate_weight,
    up_weight,
    down_weight,
):
    slots, block_length, model = tokens.shape
    moves = Moves()
    fsdp = moves.fsdp
    half = block_length // 2
    shard = model // fsdp
    attention_width = QUERY_HEADS * HEAD_SIZE
    pair_width = KEY_VALUE_HEADS * PAIR
    length = lengths[0]

    ctx = moves.where
    last = 2 * moves.ctx - 1
    block_a = jnp.where(ctx % 2 == 0, ctx, last - ctx).astype(jnp.int32)
    block_b = last - block_a
    info = jnp.stack([length, block_a, block_b]).astype(jnp.int32)
    within = jnp.arange(half, dtype=jnp.int32)
    position = jnp.concatenate([block_a * half + within, block_b * half + within])
    exponent = jnp.arange(HALF_HEAD).astype(f32) * (2.0 / HEAD_SIZE)
    phase = position.astype(f32)[:, None] * jnp.power(10000.0, -exponent)[None, :]
    cos, sin = jnp.cos(phase), jnp.sin(phase)
    cos = jnp.concatenate([cos, cos, cos, cos], -1)
    sin = jnp.concatenate([-sin, sin, -sin, sin], -1)
    valid = (position < length).astype(f32)[:, None]

    by_head = lambda w: w.reshape(shard, KEY_VALUE_HEADS, HEAD_SIZE)
    pair_weight = jnp.concatenate([by_head(key_matrix), by_head(value_matrix)], -1)
    weight_in = jnp.concatenate([query_weight, pair_weight.reshape(shard, pair_width)], 1)
    gains = jnp.concatenate([gain_one, gain_two])[None, :]
    gains = jnp.pad(gains, ((0, EXTRA - 1), (0, weight_in.shape[1] - 2 * shard)))
    in_half = shard // 2
    mine = jnp.concatenate([moves.pick(weight_in[:in_half], weight_in[in_half:]), gains], 0)
    whole_in, token = moves.gather(mine)
    whole_in = whole_in.reshape(fsdp, in_half + EXTRA, -1)
    gain_rows = whole_in[:, in_half, : 2 * shard].astype(f32)
    gain_first = gain_rows[:, :shard].reshape(1, model)
    gain_second = gain_rows[:, shard:].reshape(1, model)
    low, high = moves.both_cores(whole_in[:, :in_half])
    full_in = jnp.stack([low, high], 1).reshape(model, -1)
    full_out, token = moves.gather_rows(out_weight, token)
    ff_half = gate_weight.shape[1] // fsdp // 2
    core = moves.core.astype(jnp.int32)[None]
    own_wide = split_columns(core, gate_weight, up_weight, fsdp)
    full_wide, token = moves.gather(own_wide, token)
    own_down = moves.pick(down_weight[:ff_half], down_weight[ff_half:])
    full_down, token = moves.gather(own_down, token)
    ff_core = ff_half * fsdp

    x = moves.balance(tokens.reshape(block_length, model)).astype(f32)
    scale_one = rms_scale(x)
    normed = (x * scale_one * gain_first).astype(bf16)
    queries, pairs = project(normed, full_in, cos, sin)
    all_pairs = lax.all_gather(pairs, "ctx", axis=0, tiled=True)
    attended, log_total = attend(queries, all_pairs, info)
    hidden = x + jnp.dot(attended, full_out, preferred_element_type=f32)
    scale_two = rms_scale(hidden)
    normed_two = (hidden * scale_two * gain_second).astype(bf16)

    grad_result = valid * moves.balance(cotangent.reshape(block_length, model)).astype(f32)
    grad_low = grad_result.astype(bf16)
    both_grad = jnp.concatenate([grad_low, moves.swap(grad_low)], 0)
    both_normed = jnp.concatenate([normed_two, moves.swap(normed_two)], 0)
    wide = jnp.dot(both_normed, full_wide, preferred_element_type=f32)
    gate_pre, up_pre = wide[:, :ff_core], wide[:, ff_core:]
    sigmoid = jax.nn.sigmoid(gate_pre)
    silu = gate_pre * sigmoid
    inner = (silu * up_pre).astype(bf16)
    grad_inner = lax.dot_general(both_grad, full_down, LAST, preferred_element_type=f32)
    grad_gate_pre = grad_inner * up_pre * sigmoid * (1.0 + gate_pre * (1.0 - sigmoid))
    grad_up_pre = grad_inner * silu
    grad_wide = jnp.concatenate([grad_gate_pre.astype(bf16), grad_up_pre.astype(bf16)], 1)
    partial = lax.dot_general(grad_wide, full_wide, LAST, preferred_element_type=f32)
    grad_normed_two = partial[:block_length] + moves.swap(partial[block_length:].astype(bf16))
    partial_out = jnp.dot(inner, full_down, preferred_element_type=f32)
    result = hidden + (
        partial_out[:block_length] + moves.swap(partial_out[block_length:].astype(bf16))
    )
    output = moves.restore((valid * result).astype(bf16))
    grad_gain_two = jnp.sum(grad_normed_two * hidden * scale_two, 0)
    grad_hidden = grad_result + norm_back(grad_normed_two, hidden, scale_two, gain_second)
    hidden_low = grad_hidden.astype(bf16)
    first = (((0,), (0,)), ((), ()))
    outer = lambda a, b: lax.dot_general(a, b, first, preferred_element_type=f32).astype(bf16)
    grad_wide_weight = outer(both_normed, grad_wide).reshape(fsdp, shard, -1)
    grad_down_weight = outer(inner, both_grad).reshape(fsdp, ff_half, model)

    grad_attended = lax.dot_general(
        hidden_low, full_out, LAST, preferred_element_type=f32
    ).astype(bf16)
    grad_query_pre, pair_terms = attend_back(
        queries, grad_attended, attended, log_total, all_pairs, cos, sin, info
    )
    pair_sum = lax.psum_scatter(pair_terms, "ctx", scatter_dimension=0, tiled=True)
    grad_pair_pre = unrotate(pair_sum, cos, sin)
    grad_normed = lax.dot_general(
        grad_query_pre, full_in[:, :attention_width], LAST, preferred_element_type=f32
    ) + lax.dot_general(
        grad_pair_pre, full_in[:, attention_width:], LAST, preferred_element_type=f32
    )
    grad_gain_one = jnp.sum(grad_normed * x * scale_one, 0)
    grad_tokens = moves.restore(
        (grad_hidden + norm_back(grad_normed, x, scale_one, gain_first)).astype(bf16)
    )

    wide_part = moves.total(moves.scatter(grad_wide_weight))
    grad_gate, grad_up = merge_columns(core, wide_part, moves.swap(wide_part), fsdp)
    down_low, down_high = moves.both_cores(moves.total(moves.scatter(grad_down_weight)))
    out_parts = moves.reduce_rows(outer(attended, hidden_low))
    query_parts = moves.reduce_rows(outer(normed, grad_query_pre))
    gain_grads = jnp.stack([grad_gain_one.reshape(fsdp, shard), grad_gain_two.reshape(fsdp, shard)], 1)
    gain_grads = jnp.pad(
        gain_grads[:, :, None].astype(bf16),
        ((0, 0), (0, 0), (0, EXTRA - 1), (0, pair_width - shard)),
    )
    pair_parts = moves.reduce_rows(outer(normed, grad_pair_pre), gain_grads)

    below = lambda parts: jnp.concatenate(parts, 0).astype(f32)
    pair_grad = below([part[:in_half] for part in pair_parts])
    pair_grad = pair_grad.reshape(shard, KEY_VALUE_HEADS, PAIR)
    return (
        output.reshape(slots, block_length, model),
        grad_tokens.reshape(slots, block_length, model),
        pair_parts[0][in_half, :shard].astype(f32),
        below(query_parts),
        pair_grad[:, :, :HEAD_SIZE].reshape(shard, -1),
        pair_grad[:, :, HEAD_SIZE:].reshape(shard, -1),
        below(out_parts),
        pair_parts[1][in_half, :shard].astype(f32),
        grad_gate,
        grad_up,
        below([down_low, down_high]),
    )


def solution(mesh):
    rows, whole = P("fsdp", None), P("fsdp", "ctx", None)
    return jax.shard_map(
        local,
        mesh=mesh,
        in_specs=(
            whole, P("fsdp"), whole, P("fsdp"), rows, rows, rows, rows, P("fsdp"), rows, rows, rows,
        ),
        out_specs=(
            whole, whole, P("fsdp"), rows, rows, rows, rows, P("fsdp"), rows, rows, rows,
        ),
        check_vma=False,
    )
```

```python
import functools
import math

import jax
import jax.numpy as jnp
from jax import lax
from jax.experimental import pallas as pl
from jax.experimental.pallas import tpu as pltpu
from jax.sharding import PartitionSpec as P

QUERY_HEADS = 20
KEY_VALUE_HEADS = 5
GROUP = QUERY_HEADS // KEY_VALUE_HEADS
HEAD_SIZE = 64
PAIR = 2 * HEAD_SIZE
HALF_HEAD = HEAD_SIZE // 2
epsilon = 1e-05
LOG2E = math.log2(math.e)
SCORE_SCALE = 1.0 / math.sqrt(HEAD_SIZE)
NEGATIVE = -1e30
EXTRA = 16
f32 = jnp.float32
bf16 = jnp.bfloat16


def rms_scale(values):
    return lax.rsqrt(jnp.mean(values * values, -1, keepdims=True) + epsilon)


def norm_back(grad_normed, values, scale_rows, gain):
    weighted = grad_normed * gain
    cubed = scale_rows * scale_rows * scale_rows
    return scale_rows * weighted - values * cubed * jnp.mean(weighted * values, -1, keepdims=True)


def swap_halves(x):
    lane = lax.broadcasted_iota(jnp.int32, x.shape, 1)
    ahead = pltpu.roll(x, PAIR - HALF_HEAD, 1)
    behind = pltpu.roll(x, HALF_HEAD, 1)
    return jnp.where(lane % HEAD_SIZE < HALF_HEAD, ahead, behind)


def project_kernel(is_pair, x_ref, w_ref, cos_ref, sin_ref, out_ref):
    product = jnp.dot(x_ref[...], w_ref[...], preferred_element_type=f32)
    cos, sin = cos_ref[...], sin_ref[...]
    if is_pair:
        lane = lax.broadcasted_iota(jnp.int32, cos.shape, 1)
        cos = jnp.where(lane >= HEAD_SIZE, 1.0, cos)
        sin = jnp.where(lane >= HEAD_SIZE, 0.0, sin)
    for at in range(0, w_ref.shape[1], PAIR):
        part = product[:, at : at + PAIR]
        out_ref[:, at : at + PAIR] = (part * cos + swap_halves(part) * sin).astype(bf16)


def project(is_pair, normed, weights, cos, sin, deps=()):
    rows, model = normed.shape
    width = weights.shape[1]
    block = KEY_VALUE_HEADS * PAIR
    return pl.pallas_call(
        ignoring(functools.partial(project_kernel, is_pair), 0, len(deps)),
        grid=(width // block,),
        in_specs=anywhere(deps)
        + [
            pl.BlockSpec((rows, model), lambda i: (0, 0)),
            pl.BlockSpec((model, block), lambda i: (0, i)),
            pl.BlockSpec((rows, PAIR), lambda i: (0, 0)),
            pl.BlockSpec((rows, PAIR), lambda i: (0, 0)),
        ],
        out_specs=pl.BlockSpec((rows, block), lambda i: (0, i)),
        out_shape=jax.ShapeDtypeStruct((rows, width), bf16),
        compiler_params=pltpu.CompilerParams(vmem_limit_bytes=16 << 20),
        cost_estimate=takes(3),
        name="project",
    )(*deps, normed, weights, cos, sin)


def unrotate_kernel(x_ref, cos_ref, sin_ref, out_ref):
    lane = lax.broadcasted_iota(jnp.int32, cos_ref.shape, 1)
    cos = jnp.where(lane >= HEAD_SIZE, 1.0, cos_ref[...])
    sin = jnp.where(lane >= HEAD_SIZE, 0.0, sin_ref[...])
    for at in range(0, x_ref.shape[1], PAIR):
        part = x_ref[:, at : at + PAIR].astype(f32)
        out_ref[:, at : at + PAIR] = (part * cos - swap_halves(part) * sin).astype(bf16)


def unrotate(x, cos, sin, deps=()):
    whole = lambda v: pl.BlockSpec(v.shape, lambda i: (0, 0))
    return pl.pallas_call(
        ignoring(unrotate_kernel, 0, len(deps)),
        grid=(1,),
        in_specs=anywhere(deps) + [whole(x), whole(cos), whole(sin)],
        out_specs=whole(x),
        out_shape=jax.ShapeDtypeStruct(x.shape, bf16),
        cost_estimate=takes(3),
        name="unrotate",
    )(*deps, x, cos, sin)


def copy_kernel(core_ref, x_ref, out_ref):
    out_ref[...] = x_ref[...]


def core_rows(core, x, deps=()):
    rows, width = x.shape
    return pl.pallas_call(
        ignoring(copy_kernel, 1, len(deps)),
        grid_spec=pltpu.PrefetchScalarGridSpec(
            num_scalar_prefetch=1,
            grid=(1,),
            in_specs=anywhere(deps) + [pl.BlockSpec((rows // 2, width), lambda i, core: (core[0], 0))],
            out_specs=pl.BlockSpec((rows // 2, width), lambda i, core: (0, 0)),
        ),
        out_shape=jax.ShapeDtypeStruct((rows // 2, width), x.dtype),
        cost_estimate=takes(1),
        name="core_rows",
    )(core, *deps, x)


def block_row(block, blocks, half):
    device = jnp.minimum(block, blocks - 1 - block)
    return pl.multiple_of(device * (2 * half) + (block % 2) * half, half)


def two_blocks(ref, step, blocks, half):
    first = ref[pl.ds(block_row(2 * step, blocks, half), half), :]
    second = ref[pl.ds(block_row(2 * step + 1, blocks, half), half), :]
    return jnp.concatenate([first, second], 0)


def one_head(ref, rows, head, low):
    part = ref[rows, (head // 2) * PAIR : (head // 2 + 1) * PAIR].astype(f32)
    lane = lax.broadcasted_iota(jnp.int32, part.shape, 1)
    if (head % 2 == 0) != low:
        part = pltpu.roll(part, HEAD_SIZE, 1)
    keep = lane < HEAD_SIZE if low else lane >= HEAD_SIZE
    return jnp.where(keep, part, 0.0).astype(bf16)


def allowed_keys(step, block, length, half):
    shape = (2 * half, half)
    key_pos = lax.broadcasted_iota(jnp.int32, shape, 0) + step * (2 * half)
    query_pos = lax.broadcasted_iota(jnp.int32, shape, 1) + block * half
    return key_pos <= jnp.minimum(query_pos, length - 1)


def key_steps(block, length, half):
    keys = jnp.minimum((block + 1) * half, length)
    return (keys + 2 * half - 1) // (2 * half)


LAST = (((1,), (1,)), ((), ()))


def ignoring(kernel, scalars, count):
    def body(*refs):
        return kernel(*refs[:scalars], *refs[scalars + count :])

    return body


def anywhere(deps):
    return [pl.BlockSpec(memory_space=pl.ANY)] * len(deps)


def takes(microseconds):
    return pl.CostEstimate(
        flops=int(microseconds * 0.45e9 * 1.1535), bytes_accessed=0, transcendentals=0
    )


def copy_all_kernel(x_ref, out_ref):
    out_ref[...] = x_ref[...]


def copy_later(x, deps):
    whole = pl.BlockSpec(x.shape, lambda i: (0, 0))
    return pl.pallas_call(
        ignoring(copy_all_kernel, 0, len(deps)),
        grid=(1,),
        in_specs=anywhere(deps) + [whole],
        out_specs=whole,
        out_shape=jax.ShapeDtypeStruct(x.shape, x.dtype),
        cost_estimate=takes(1),
        name="copy_later",
    )(*deps, x)


def nothing_kernel(*refs):
    pass


def gate(values, *deps):
    values = tuple(values)
    count = len(deps)
    return pl.pallas_call(
        nothing_kernel,
        in_specs=anywhere(deps) + anywhere(values),
        out_specs=anywhere(values),
        out_shape=[jax.ShapeDtypeStruct(v.shape, v.dtype) for v in values],
        input_output_aliases={count + i: i for i in range(len(values))},
        cost_estimate=takes(0),
        name="gate",
    )(*deps, *values)


def forward_kernel(blocks, info_ref, q_ref, kv_ref, o_ref, lse_ref, q_sc, m_sc, l_sc, acc_sc):
    half = q_ref.shape[0] // 2
    wide = GROUP * half
    length = info_ref[0]
    scale = SCORE_SCALE * LOG2E
    for slot in range(2):
        block = info_ref[1 + slot]
        rows = slice(slot * half, (slot + 1) * half)
        for head in range(GROUP):
            q_sc[:, head * half : (head + 1) * half] = one_head(q_ref, rows, head, True).T
        m_sc[...] = jnp.full_like(m_sc, NEGATIVE)
        l_sc[...] = jnp.zeros_like(l_sc)
        acc_sc[...] = jnp.zeros_like(acc_sc)

        def work(step, masked):
            pair = two_blocks(kv_ref, step, blocks, half)
            values_t = pair.T[HEAD_SIZE:]
            if masked:
                allowed = allowed_keys(step, block, length, half)
                allowed = jnp.concatenate([allowed, allowed], 1)
            sides = [slice(i * wide // 2, (i + 1) * wide // 2) for i in range(2)]
            both = [jnp.dot(pair, q_sc[:, at], preferred_element_type=f32) for at in sides]
            for at, scores in zip(sides, both):
                if masked:
                    scores = jnp.where(allowed, scores, NEGATIVE)
                m_old = m_sc[:1, at]
                m_new = jnp.maximum(m_old, jnp.max(scores, 0, keepdims=True) * scale)
                weights = jnp.exp2(scores * scale - m_new)
                fading = jnp.exp2(m_old - m_new)
                m_sc[:1, at] = m_new
                sums = jnp.sum(weights.reshape(2 * half // 8, 8, wide // 2), 0)
                l_sc[:, at] = l_sc[:, at] * fading + sums
                acc_sc[:, at] = acc_sc[:, at] * fading + jnp.dot(
                    values_t, weights.astype(bf16), preferred_element_type=f32
                )

        steps = key_steps(block, length, half)

        @pl.loop(0, steps - 1)
        def _(step):
            work(step, False)

        work(steps - 1, True)
        total = jnp.sum(l_sc[...], 0, keepdims=True)
        result = acc_sc[...] / total
        lse = m_sc[:1] + jnp.log2(total)
        for at in range(0, GROUP, 2):
            two = [result[:, head * half : (head + 1) * half] for head in (at, at + 1)]
            o_ref[rows, at * HEAD_SIZE : (at + 2) * HEAD_SIZE] = (
                jnp.concatenate(two, 0).T.astype(bf16)
            )
        for head in range(GROUP):
            lse_ref[0, head : head + 1, rows] = lse[:, head * half : (head + 1) * half]


def attend(head, count, grown, q, pairs, info, deps=()):
    rows, keys = q.shape[0], pairs.shape[0]
    half = rows // 2
    wide = GROUP * half
    width = GROUP * HEAD_SIZE
    aliases = {1 + i: i for i in range(len(grown))}
    deps = tuple(grown) + tuple(deps)
    return pl.pallas_call(
        ignoring(functools.partial(forward_kernel, keys // half), 1, len(deps)),
        grid_spec=pltpu.PrefetchScalarGridSpec(
            num_scalar_prefetch=1,
            grid=(count,),
            in_specs=anywhere(deps)
            + [
                pl.BlockSpec((rows, width), lambda g, info: (0, head + g)),
                pl.BlockSpec((keys, PAIR), lambda g, info: (0, head + g)),
            ],
            out_specs=[
                pl.BlockSpec((rows, width), lambda g, info: (0, head + g)),
                pl.BlockSpec((1, GROUP, rows), lambda g, info: (head + g, 0, 0)),
            ],
            scratch_shapes=[
                pltpu.VMEM((PAIR, wide), bf16),
                pltpu.VMEM((8, wide), f32),
                pltpu.VMEM((8, wide), f32),
                pltpu.VMEM((HEAD_SIZE, wide), f32),
            ],
        ),
        out_shape=[
            jax.ShapeDtypeStruct(q.shape, bf16),
            jax.ShapeDtypeStruct((KEY_VALUE_HEADS, GROUP, rows), f32),
        ],
        input_output_aliases=aliases,
        compiler_params=pltpu.CompilerParams(vmem_limit_bytes=20 << 20),
        cost_estimate=takes(10 * count),
        name="attend",
    )(info, *deps, q, pairs)


def backward_kernel(
    blocks, info_ref, q_ref, do_ref, o_ref, lse_ref, kv_ref, cos_ref, sin_ref,
    dq_ref, same_ref, other_ref, both_sc, q_sc, do_sc, row_sc, dq_sc, dkv_sc, terms_sc,
):
    half = q_ref.shape[0] // 2
    wide = GROUP * half
    length = info_ref[0]
    dkv_sc[...] = jnp.zeros_like(dkv_sc)
    for slot in range(2):
        block = info_ref[1 + slot]
        rows = slice(slot * half, (slot + 1) * half)
        for head in range(GROUP):
            at = slice(head * half, (head + 1) * half)
            query = one_head(q_ref, rows, head, True)
            grad = one_head(do_ref, rows, head, False)
            both_sc[head * half : (head + 1) * half] = query
            both_sc[wide + head * half : wide + (head + 1) * half] = grad
            q_sc[:, at] = query.T
            do_sc[:, at] = grad.T
            row_sc[1:2, at] = lse_ref[0, head : head + 1, rows]
        for at in range(0, GROUP, 2):
            lanes = slice(at * HEAD_SIZE, (at + 2) * HEAD_SIZE)
            product = (do_ref[rows, lanes].astype(f32) * o_ref[rows, lanes].astype(f32)).T
            for i in range(2):
                row_sc[:1, (at + i) * half : (at + i + 1) * half] = jnp.sum(
                    product[i * HEAD_SIZE : (i + 1) * HEAD_SIZE], 0, keepdims=True
                )
        dq_sc[...] = jnp.zeros_like(dq_sc)

        def work(step, masked):
            pair = two_blocks(kv_ref, step, blocks, half)
            keys_t = pair.T[:HEAD_SIZE]
            if masked:
                allowed = allowed_keys(step, block, length, half)
            sides = [slice(head * half, (head + 1) * half) for head in range(GROUP)]

            def products(at):
                return (
                    jnp.dot(pair, q_sc[:, at], preferred_element_type=f32),
                    jnp.dot(pair, do_sc[:, at], preferred_element_type=f32),
                )

            coming = products(sides[0])
            for head, at in enumerate(sides):
                scores, grad_probs = coming
                if head + 1 < GROUP:
                    coming = products(sides[head + 1])
                probs = jnp.exp2(scores * (SCORE_SCALE * LOG2E) - row_sc[1:2, at])
                if masked:
                    probs = jnp.where(allowed, probs, 0.0)
                grad_scores = (probs * (grad_probs - row_sc[:1, at])).astype(bf16)
                terms_sc[:, at] = grad_scores
                terms_sc[:, wide + head * half : wide + (head + 1) * half] = probs.astype(bf16)
                dq_sc[:, at] += jnp.dot(keys_t, grad_scores, preferred_element_type=f32)
            update = jnp.dot(terms_sc[...], both_sc[...], preferred_element_type=f32)
            for i in range(2):
                at = pl.ds(block_row(2 * step + i, blocks, half), half)
                dkv_sc[at, :] += update[i * half : (i + 1) * half]

        steps = key_steps(block, length, half)

        @pl.loop(0, steps - 1)
        def _(step):
            work(step, False)

        work(steps - 1, True)
        for at in range(0, GROUP, 2):
            two = [dq_sc[:, head * half : (head + 1) * half] for head in (at, at + 1)]
            grad = jnp.concatenate(two, 0).T * SCORE_SCALE
            grad = grad * cos_ref[rows, :] - swap_halves(grad) * sin_ref[rows, :]
            dq_ref[rows, at * HEAD_SIZE : (at + 2) * HEAD_SIZE] = grad.astype(bf16)
    lane = lax.broadcasted_iota(jnp.int32, (2 * half, PAIR), 1)
    scale = jnp.where(lane < HEAD_SIZE, SCORE_SCALE, 1.0)
    core = info_ref[3]
    for i in range(blocks // 4):
        rows = slice(i * 2 * half, (i + 1) * 2 * half)
        for ref, side in ((same_ref, core), (other_ref, 1 - core)):
            at = pl.ds(pl.multiple_of((2 * i + side) * 2 * half, 2 * half), 2 * half)
            ref[rows, :] = (dkv_sc[at, :] * scale).astype(bf16)


def attend_back(head, span, grown, q, grad, attended, lse, pairs, cos, sin, info, deps=()):
    rows, keys = q.shape[0], pairs.shape[0]
    half = rows // 2
    wide = GROUP * half
    width = GROUP * HEAD_SIZE
    filled = [at for at, value in enumerate(grown) if value is not None]
    aliases = {1 + i: at for i, at in enumerate(filled)}
    deps = tuple(grown[at] for at in filled) + tuple(deps)
    head_block = pl.BlockSpec((rows, width), lambda g, info: (0, head))
    half_block = pl.BlockSpec((keys // 2, PAIR), lambda g, info: (0, head - span[0]))
    table = pl.BlockSpec((rows, PAIR), lambda g, info: (0, 0))
    half_shape = jax.ShapeDtypeStruct((keys // 2, span[1] * PAIR), bf16)
    return pl.pallas_call(
        ignoring(functools.partial(backward_kernel, keys // half), 1, len(deps)),
        grid_spec=pltpu.PrefetchScalarGridSpec(
            num_scalar_prefetch=1,
            grid=(1,),
            in_specs=anywhere(deps)
            + [
                head_block,
                head_block,
                head_block,
                pl.BlockSpec((1, GROUP, rows), lambda g, info: (head, 0, 0)),
                pl.BlockSpec((keys, PAIR), lambda g, info: (0, head)),
                table,
                table,
            ],
            out_specs=[head_block, half_block, half_block],
            scratch_shapes=[
                pltpu.VMEM((2 * wide, PAIR), bf16),
                pltpu.VMEM((PAIR, wide), bf16),
                pltpu.VMEM((PAIR, wide), bf16),
                pltpu.VMEM((8, wide), f32),
                pltpu.VMEM((HEAD_SIZE, wide), f32),
                pltpu.VMEM((keys, PAIR), f32),
                pltpu.VMEM((2 * half, 2 * wide), bf16),
            ],
        ),
        out_shape=[jax.ShapeDtypeStruct(q.shape, bf16), half_shape, half_shape],
        input_output_aliases=aliases,
        compiler_params=pltpu.CompilerParams(vmem_limit_bytes=24 << 20),
        cost_estimate=takes(16),
        name="attend_back",
    )(info, *deps, q, grad, attended, lse, pairs, cos, sin)


def outer_kernel(parts, core_ref, a_ref, b_ref, keep_ref, send_ref, at_sc):
    @pl.when(pl.program_id(0) == 0)
    def _():
        at_sc[...] = a_ref[...].T

    rows = at_sc.shape[0] // parts // 2
    for i in range(parts):
        for side, ref in enumerate((keep_ref, send_ref)):
            half = jnp.bitwise_xor(core_ref[0], side)
            start = pl.multiple_of((2 * i + half) * rows, 16)
            ref[i] = jnp.dot(
                at_sc[pl.ds(start, rows), :], b_ref[...], preferred_element_type=f32
            ).astype(bf16)


def outer_rows(core, a, b, parts, deps=()):
    tokens, model = a.shape
    width = b.shape[1]
    block = KEY_VALUE_HEADS * PAIR
    rows = model // parts // 2
    out = jax.ShapeDtypeStruct((parts, rows, width), bf16)
    spec = pl.BlockSpec((parts, rows, block), lambda i, core: (0, 0, i))
    return pl.pallas_call(
        ignoring(functools.partial(outer_kernel, parts), 1, len(deps)),
        grid_spec=pltpu.PrefetchScalarGridSpec(
            num_scalar_prefetch=1,
            grid=(width // block,),
            in_specs=anywhere(deps)
            + [
                pl.BlockSpec((tokens, model), lambda i, core: (0, 0)),
                pl.BlockSpec((tokens, block), lambda i, core: (0, i)),
            ],
            out_specs=[spec, spec],
            scratch_shapes=[pltpu.VMEM((model, tokens), bf16)],
        ),
        out_shape=[out, out],
        compiler_params=pltpu.CompilerParams(vmem_limit_bytes=20 << 20),
        cost_estimate=takes(3),
        name="outer_rows",
    )(core, *deps, a, b)


def place_kernel(count, spots_ref, *refs):
    out_ref, sems = refs[count], refs[count + 1]
    copies = []
    for i, ref in enumerate(refs[:count]):
        start = pl.multiple_of(spots_ref[i], 16)
        copy = pltpu.make_async_copy(ref, out_ref.at[pl.ds(start, ref.shape[0])], sems.at[i])
        copy.start()
        copies.append(copy)
    for copy in copies:
        copy.wait()


def place(pieces, spots, rows):
    count = len(pieces)
    width = pieces[0].shape[1]
    return pl.pallas_call(
        functools.partial(place_kernel, count),
        grid_spec=pltpu.PrefetchScalarGridSpec(
            num_scalar_prefetch=1,
            grid=(1,),
            in_specs=anywhere(pieces),
            out_specs=pl.BlockSpec((rows, width), lambda i, spots: (0, 0)),
            scratch_shapes=[pltpu.SemaphoreType.DMA((count,))],
        ),
        out_shape=jax.ShapeDtypeStruct((rows, width), pieces[0].dtype),
        compiler_params=pltpu.CompilerParams(vmem_limit_bytes=24 << 20),
        cost_estimate=takes(3),
        name="place",
    )(jnp.stack(spots).astype(jnp.int32), *pieces)


def split_kernel(parts, core_ref, gate_ref, up_ref, out_ref):
    width = gate_ref.shape[1] // parts // 2
    for core in range(2):

        @pl.when(core_ref[0] == core)
        def _():
            taken = []
            for ref in (gate_ref, up_ref):
                for i in range(parts):
                    at = (2 * i + core) * width
                    taken.append(ref[:, at : at + width])
            out_ref[...] = jnp.concatenate(taken, 1)


def split_columns(core, gate, up, parts, deps=()):
    rows, width = gate.shape
    block = rows // 2
    spec = pl.BlockSpec((block, width), lambda i, core: (i, 0))
    return pl.pallas_call(
        ignoring(functools.partial(split_kernel, parts), 1, len(deps)),
        grid_spec=pltpu.PrefetchScalarGridSpec(
            num_scalar_prefetch=1,
            grid=(2,),
            in_specs=anywhere(deps) + [spec, spec],
            out_specs=spec,
        ),
        out_shape=jax.ShapeDtypeStruct((rows, width), gate.dtype),
        cost_estimate=takes(3.5),
        name="split_columns",
    )(core, *deps, gate, up)


def merge_kernel(parts, core_ref, own_ref, other_ref, out_ref):
    width = own_ref.shape[1] // parts
    for core in range(2):

        @pl.when(core_ref[0] == core)
        def _():
            taken = []
            for i in range(parts):
                for ref in (own_ref, other_ref) if core == 0 else (other_ref, own_ref):
                    taken.append(ref[:, i * width : (i + 1) * width].astype(f32))
            out_ref[...] = jnp.concatenate(taken, 1)


def merge_columns(core, own, other, parts):
    rows, width = own.shape
    block = rows // 4 if rows % 64 == 0 else rows // 2
    spec = pl.BlockSpec((block, width), lambda i, core: (i, 0))
    return pl.pallas_call(
        functools.partial(merge_kernel, parts),
        grid_spec=pltpu.PrefetchScalarGridSpec(
            num_scalar_prefetch=1,
            grid=(rows // block,),
            in_specs=[spec, spec],
            out_specs=pl.BlockSpec((block, 2 * width), lambda i, core: (i, 0)),
        ),
        out_shape=jax.ShapeDtypeStruct((rows, 2 * width), f32),
        compiler_params=pltpu.CompilerParams(vmem_limit_bytes=24 << 20),
        cost_estimate=takes(2.7),
        name="merge_columns",
    )(core, own, other)


def after(value, *others):
    return lax.optimization_barrier((value,) + others)[0]


class Moves:
    def __init__(self):
        self.ctx, self.fsdp = lax.axis_size("ctx"), lax.axis_size("fsdp")
        self.me, self.where = lax.axis_index("fsdp"), lax.axis_index("ctx")
        self.core = self.where % 2
        self.square = self.fsdp == 4
        self.line = self.ctx == 8

    def across(self, value, bit):
        return lax.ppermute(value, "fsdp", [(i, i ^ bit) for i in range(self.fsdp)])

    def swap(self, value):
        return lax.ppermute(value, "ctx", [(i, i ^ 1) for i in range(self.ctx)])

    def pick(self, low, high):
        return jnp.where(self.core == 0, low, high)

    def owner(self, half):
        return half if half < self.ctx else 2 * self.ctx - 1 - half

    def balance(self, rows):
        half = rows.shape[0] // 2
        return jnp.concatenate(
            [
                lax.ppermute(
                    rows[i * half : (i + 1) * half],
                    "ctx",
                    [(d, self.owner(2 * d + i)) for d in range(self.ctx)],
                )
                for i in range(2)
            ],
            0,
        )

    def restore(self, rows):
        half = rows.shape[0] // 2
        return jnp.concatenate(
            [
                lax.ppermute(
                    rows[i * half : (i + 1) * half],
                    "ctx",
                    [(self.owner(2 * d + i), d) for d in range(self.ctx)],
                )
                for i in range(2)
            ],
            0,
        )

    def gather_all(self, own):
        return lax.all_gather(own, "fsdp", axis=0, tiled=True)

    def gather_first(self, own):
        return (self.across(own, 1), self.across(own, 2)) if self.square else ()

    def gather_last(self, own, arrived):
        if not self.square:
            return self.gather_all(own)
        rows = own.shape[0]
        half = rows // 32 * 16
        by_x, by_y = arrived
        top, bottom = self.across(by_x[:half], 2), self.across(by_y[half:], 1)
        me = self.me
        spots = [me * rows, (me ^ 1) * rows, (me ^ 2) * rows, (me ^ 3) * rows, (me ^ 3) * rows + half]
        return place([own, by_x, by_y, top, bottom], spots, 4 * rows)

    def chip(self, value, bit):
        return lax.ppermute(value, "ctx", [(i, i ^ (2 * bit)) for i in range(self.ctx)])

    def gather_pairs(self, pairs):
        if not self.line:
            return lax.all_gather(pairs, "ctx", axis=0, tiled=True)
        rows = pairs.shape[0]
        pieces, spots = [], []
        for bit in (0, 3, 2, 1):
            piece = pairs if bit == 0 else self.chip(pairs, bit)
            pieces += [piece, self.swap(piece)]
            spots += [(self.where ^ (2 * bit)) * rows, (self.where ^ (2 * bit + 1)) * rows]
        return place(pieces, spots, self.ctx * rows)

    def scatter_pairs(self, kept):
        groups = [list(range(c, self.ctx, 2)) for c in range(2)]
        return lax.psum_scatter(
            kept, "ctx", scatter_dimension=0, axis_index_groups=groups, tiled=True
        )

    def scatter_at_once(self, whole):
        if not self.square:
            rows = whole.shape[1]
            flat = whole.reshape(self.fsdp * rows, -1)
            return lax.psum_scatter(flat, "fsdp", scatter_dimension=0, tiled=True), ()
        part = lambda bit: lax.dynamic_index_in_dim(whole, self.me ^ bit, 0, keepdims=False)
        moved = [self.across(part(bit), bit) for bit in (3, 1, 2)]
        wide = [value.astype(f32) for value in moved]
        total = (part(0).astype(f32) + wide[0]) + (wide[1] + wide[2])
        return total.astype(bf16), tuple(moved)

    def total_at_once(self, part):
        if not self.line:
            return self.over_line(part)
        moved = [part] + [self.chip(part, bit) for bit in (1, 2, 3)]
        z = self.where // 2
        low = lambda a, b: jnp.where(z % 2 == 0, a, b).astype(f32)
        near = low(moved[0], moved[1]) + low(moved[1], moved[0])
        far = low(moved[2], moved[3]) + low(moved[3], moved[2])
        first = jnp.where(z // 2 == 0, near, far)
        second = jnp.where(z // 2 == 0, far, near)
        return (first + second).astype(bf16)

    def over_line(self, part):
        groups = [list(range(c, self.ctx, 2)) for c in range(2)]
        return lax.psum(part, "ctx", axis_index_groups=groups)

    def along(self, value, pairs):
        return lax.ppermute(
            value, "ctx", [(2 * a + c, 2 * b + c) for a, b in pairs for c in range(2)]
        )

    def inward(self, part):
        return (self.along(part, [(0, 1), (3, 2)]),) if self.line else ()

    def crossing(self, part, arrived):
        if not self.line:
            return part, ()
        inner = part + arrived[0]
        return inner, (self.along(inner, [(1, 2), (2, 1)]),)

    def outward(self, inner, arrived):
        if not self.line:
            return inner, ()
        summed = inner + arrived[0]
        return summed, (self.along(summed, [(1, 0), (2, 3)]),)

    def settled(self, summed, arrived):
        if not self.line:
            return self.over_line(summed)
        z = self.where // 2
        return jnp.where((z == 0) | (z == 3), arrived[0], summed)

    def both_cores(self, part):
        other = self.swap(part)
        return self.pick(part, other), self.pick(other, part)


def local(
    tokens,
    lengths,
    cotangent,
    gain_one,
    query_weight,
    key_matrix,
    value_matrix,
    out_weight,
    gain_two,
    gate_weight,
    up_weight,
    down_weight,
):
    slots, block_length, model = tokens.shape
    moves = Moves()
    fsdp = moves.fsdp
    half = block_length // 2
    shard = model // fsdp
    attention_width = QUERY_HEADS * HEAD_SIZE
    pair_width = KEY_VALUE_HEADS * PAIR
    length = lengths[0]

    ctx = moves.where
    last = 2 * moves.ctx - 1
    block_a = jnp.where(ctx % 2 == 0, ctx, last - ctx).astype(jnp.int32)
    block_b = last - block_a
    info = jnp.stack([length, block_a, block_b, moves.core]).astype(jnp.int32)
    within = jnp.arange(half, dtype=jnp.int32)
    position = jnp.concatenate([block_a * half + within, block_b * half + within])
    exponent = jnp.arange(HALF_HEAD).astype(f32) * (2.0 / HEAD_SIZE)
    phase = position.astype(f32)[:, None] * jnp.power(10000.0, -exponent)[None, :]
    cos, sin = jnp.cos(phase), jnp.sin(phase)
    cos = jnp.concatenate([cos, cos, cos, cos], -1)
    sin = jnp.concatenate([-sin, sin, -sin, sin], -1)
    valid = (position < length).astype(f32)[:, None]

    core = moves.core.astype(jnp.int32)[None]
    in_half = shard // 2
    by_head = lambda w: w.reshape(shard, KEY_VALUE_HEADS, HEAD_SIZE)
    pair_weight = jnp.concatenate([by_head(key_matrix), by_head(value_matrix)], -1)
    pair_weight = pair_weight.reshape(shard, pair_width)
    gains = jnp.concatenate([gain_one, gain_two])[None, :]
    gains = jnp.pad(gains, ((0, EXTRA - 1), (0, pair_width - 2 * shard)))
    own_pair = jnp.concatenate([moves.pick(pair_weight[:in_half], pair_weight[in_half:]), gains], 0)
    x = moves.balance(tokens.reshape(block_length, model)).astype(f32)
    arrived = moves.gather_first(own_pair)
    own_query = core_rows(core, query_weight)
    whole_query = moves.gather_all(own_query)
    whole_pair = moves.gather_last(own_pair, arrived)
    whole_pair = whole_pair.reshape(fsdp, in_half + EXTRA, pair_width)
    gain_rows = whole_pair[:, in_half, : 2 * shard].astype(f32)
    gain_first = gain_rows[:, :shard].reshape(1, model)
    gain_second = gain_rows[:, shard:].reshape(1, model)
    beside = lambda two: jnp.stack(two, 1).reshape(model, -1)
    full_pair = beside(moves.both_cores(whole_pair[:, :in_half]))
    own_wide = split_columns(core, gate_weight, up_weight, fsdp)
    wide_arrived = moves.gather_first(own_wide)

    scale_one = rms_scale(x)
    normed = (x * scale_one * gain_first).astype(bf16)
    pairs = project(True, normed, full_pair, cos, sin)
    all_pairs = lax.all_gather(pairs, "ctx", axis=0, tiled=True)
    (whole_query,) = gate((whole_query,), pairs)
    full_query = beside(moves.both_cores(whole_query.reshape(fsdp, in_half, -1)))
    queries = project(False, normed, full_query, cos, sin)
    own_out = core_rows(core, out_weight, (queries,))
    whole_out = moves.gather_all(own_out)
    own_down = core_rows(core, down_weight, (own_out,))
    full_down = moves.gather_all(own_down)
    if wide_arrived:
        wide_arrived = gate(wide_arrived, queries)
    full_wide = moves.gather_last(own_wide, wide_arrived)
    late = copy_later(cotangent.reshape(block_length, model), (all_pairs, queries))
    cotangent_rows = moves.balance(late)
    ff_half = gate_weight.shape[1] // fsdp // 2
    ff_core = ff_half * fsdp
    grown = attend(0, 3, (), queries, all_pairs, info, (own_down, late))
    (whole_out,) = gate((whole_out,), grown[1])
    out_cores = moves.both_cores(whole_out.reshape(fsdp, in_half, model))
    full_out = beside(out_cores)
    attended, log_total = attend(
        3, 2, grown, queries, all_pairs, info, (cotangent_rows, full_wide)
    )
    hidden = x + jnp.dot(attended, full_out, preferred_element_type=f32)
    scale_two = rms_scale(hidden)
    normed_two = (hidden * scale_two * gain_second).astype(bf16)

    grad_result = valid * cotangent_rows.astype(f32)
    grad_low = grad_result.astype(bf16)
    both_grad = jnp.concatenate([grad_low, moves.swap(grad_low)], 0)
    both_normed = jnp.concatenate([normed_two, moves.swap(normed_two)], 0)
    wide = jnp.dot(both_normed, full_wide, preferred_element_type=f32)
    gate_pre, up_pre = wide[:, :ff_core], wide[:, ff_core:]
    sigmoid = jax.nn.sigmoid(gate_pre)
    silu = gate_pre * sigmoid
    inner = (silu * up_pre).astype(bf16)
    grad_inner = lax.dot_general(both_grad, full_down, LAST, preferred_element_type=f32)
    grad_gate_pre = grad_inner * up_pre * sigmoid * (1.0 + gate_pre * (1.0 - sigmoid))
    grad_up_pre = grad_inner * silu
    grad_wide = jnp.concatenate([grad_gate_pre.astype(bf16), grad_up_pre.astype(bf16)], 1)
    first = (((0,), (0,)), ((), ()))
    outer = lambda a, b: lax.dot_general(a, b, first, preferred_element_type=f32).astype(bf16)
    partial = lax.dot_general(grad_wide, full_wide, LAST, preferred_element_type=f32)
    grad_normed_two = partial[:block_length] + moves.swap(partial[block_length:].astype(bf16))
    grad_gain_two = jnp.sum(grad_normed_two * hidden * scale_two, 0)
    grad_hidden = grad_result + norm_back(grad_normed_two, hidden, scale_two, gain_second)
    hidden_low = grad_hidden.astype(bf16)
    shared = lambda grad: lax.psum_scatter(grad, "fsdp", scatter_dimension=0, tiled=True)
    gate_terms = outer(both_normed, grad_wide[:, :ff_core])
    up_terms = outer(both_normed, grad_wide[:, ff_core:])
    gate_shared, up_shared = shared(gate_terms), shared(up_terms)

    grad_attended = lax.dot_general(
        hidden_low, full_out, LAST, preferred_element_type=f32
    ).astype(bf16)

    def back(head, span, grown, *deps):
        return attend_back(
            head, span, grown, queries, grad_attended, attended, log_total, all_pairs, cos, sin,
            info, deps,
        )

    span = (0, KEY_VALUE_HEADS)
    grown = back(0, span, (None, None, None), gate_terms, up_terms)
    (inner,) = gate((inner,), grown[0])
    partial_out = jnp.dot(inner, full_down, preferred_element_type=f32)
    grown = back(1, span, grown, partial_out)
    result = hidden + (
        partial_out[:block_length] + moves.swap(partial_out[block_length:].astype(bf16))
    )
    output = moves.restore((valid * result).astype(bf16))
    down_terms = outer(inner, both_grad)
    down_shared = shared(down_terms)
    gate_in = moves.inward(gate_shared)
    grown = back(2, span, grown, down_terms, gate_shared)
    grown = back(3, span, grown)
    gate_inner, gate_across = moves.crossing(gate_shared, gate_in)
    grown = back(4, span, grown, output, *gate_in)
    grad_query_pre, same, other = grown

    pair_sum = moves.scatter_pairs(same + moves.swap(other))
    up_shared, down_shared = gate((up_shared, down_shared), grad_query_pre)
    up_in = moves.inward(up_shared)
    down_in = moves.inward(down_shared)
    gate_sum, gate_out = moves.outward(gate_inner, gate_across)
    from_out = outer_rows(core, attended, hidden_low, fsdp, (grad_query_pre,))
    from_query = outer_rows(core, normed, grad_query_pre, fsdp)
    square = [jnp.concatenate(two, 2) for two in zip(from_out, from_query)]
    square_shared = shared((square[0] + moves.swap(square[1])).reshape(model // 2, -1))
    by_query = lax.dot_general(grad_query_pre, full_query, LAST, preferred_element_type=f32)

    up_inner, up_across = moves.crossing(up_shared, up_in)
    down_inner, down_across = moves.crossing(down_shared, down_in)
    grad_pair_pre = unrotate(pair_sum, cos, sin, (by_query,) + up_in + down_in + gate_out)
    by_pair = lax.dot_general(grad_pair_pre, full_pair, LAST, preferred_element_type=f32)
    from_pair = outer_rows(core, normed, grad_pair_pre, fsdp)
    grad_normed = by_query + by_pair
    grad_gain_one = jnp.sum(grad_normed * x * scale_one, 0)
    grad_tokens = (grad_hidden + norm_back(grad_normed, x, scale_one, gain_first)).astype(bf16)
    gain_grads = jnp.stack([grad_gain_one.reshape(fsdp, shard), grad_gain_two.reshape(fsdp, shard)], 1)
    gain_grads = jnp.pad(
        gain_grads[:, :, None].astype(bf16),
        ((0, 0), (0, 0), (0, EXTRA - 1), (0, pair_width - shard)),
    )
    mine_too = moves.pick(gain_grads[:, 0], gain_grads[:, 1])
    others_too = moves.pick(gain_grads[:, 1], gain_grads[:, 0])
    keep = jnp.concatenate([from_pair[0], mine_too], 1)
    send = jnp.concatenate([from_pair[1], others_too], 1)
    pair_shared = shared((keep + moves.swap(send)).reshape(fsdp * (in_half + EXTRA), -1))
    pair_part = moves.over_line(pair_shared)
    square_part = moves.over_line(square_shared)
    grad_tokens = moves.restore(grad_tokens)

    gate_part = moves.settled(gate_sum, gate_out)
    gate_other = moves.swap(gate_part)
    up_sum, up_out = moves.outward(up_inner, up_across)
    grad_gate = merge_columns(core, gate_part, gate_other, fsdp)
    up_part = moves.settled(up_sum, up_out)
    grad_up = merge_columns(core, up_part, moves.swap(up_part), fsdp)
    down_sum, down_out = moves.outward(down_inner, down_across)
    down_low, down_high = moves.both_cores(moves.settled(down_sum, down_out))
    pair_parts = moves.both_cores(pair_part)
    square_parts = moves.both_cores(square_part)

    below = lambda parts: jnp.concatenate(parts, 0).astype(f32)
    pair_grad = below([part[:in_half] for part in pair_parts])
    pair_grad = pair_grad.reshape(shard, KEY_VALUE_HEADS, PAIR)
    return (
        output.reshape(slots, block_length, model),
        grad_tokens.reshape(slots, block_length, model),
        pair_parts[0][in_half, :shard].astype(f32),
        below([part[:, model:] for part in square_parts]),
        pair_grad[:, :, :HEAD_SIZE].reshape(shard, -1),
        pair_grad[:, :, HEAD_SIZE:].reshape(shard, -1),
        below([part[:, :model] for part in square_parts]),
        pair_parts[1][in_half, :shard].astype(f32),
        grad_gate,
        grad_up,
        below([down_low, down_high]),
    )


def solution(mesh):
    rows, whole = P("fsdp", None), P("fsdp", "ctx", None)
    return jax.shard_map(
        local,
        mesh=mesh,
        in_specs=(
            whole, P("fsdp"), whole, P("fsdp"), rows, rows, rows, rows, P("fsdp"), rows, rows, rows,
        ),
        out_specs=(
            whole, whole, P("fsdp"), rows, rows, rows, rows, P("fsdp"), rows, rows, rows,
        ),
        check_vma=False,
    )
```

```python
import functools
import math

import jax
import jax.numpy as jnp
from jax import lax
from jax.experimental import pallas as pl
from jax.experimental.pallas import tpu as pltpu
from jax.sharding import PartitionSpec as P

QUERY_HEADS = 20
KEY_VALUE_HEADS = 5
GROUP = QUERY_HEADS // KEY_VALUE_HEADS
HEAD_SIZE = 64
PAIR = 2 * HEAD_SIZE
HALF_HEAD = HEAD_SIZE // 2
epsilon = 1e-05
LOG2E = math.log2(math.e)
SCORE_SCALE = 1.0 / math.sqrt(HEAD_SIZE)
NEGATIVE = -1e30
EXTRA = 16
f32 = jnp.float32
bf16 = jnp.bfloat16


def rms_scale(values):
    return lax.rsqrt(jnp.mean(values * values, -1, keepdims=True) + epsilon)


def norm_back(grad_normed, values, scale_rows, gain):
    weighted = grad_normed * gain
    cubed = scale_rows * scale_rows * scale_rows
    return scale_rows * weighted - values * cubed * jnp.mean(weighted * values, -1, keepdims=True)


def swap_halves(x):
    lane = lax.broadcasted_iota(jnp.int32, x.shape, 1)
    ahead = pltpu.roll(x, PAIR - HALF_HEAD, 1)
    behind = pltpu.roll(x, HALF_HEAD, 1)
    return jnp.where(lane % HEAD_SIZE < HALF_HEAD, ahead, behind)


def project_kernel(is_pair, x_ref, w_ref, cos_ref, sin_ref, out_ref):
    product = jnp.dot(x_ref[...], w_ref[...], preferred_element_type=f32)
    cos, sin = cos_ref[...], sin_ref[...]
    if is_pair:
        lane = lax.broadcasted_iota(jnp.int32, cos.shape, 1)
        cos = jnp.where(lane >= HEAD_SIZE, 1.0, cos)
        sin = jnp.where(lane >= HEAD_SIZE, 0.0, sin)
    for at in range(0, w_ref.shape[1], PAIR):
        part = product[:, at : at + PAIR]
        out_ref[:, at : at + PAIR] = (part * cos + swap_halves(part) * sin).astype(bf16)


def project(is_pair, normed, weights, cos, sin, deps=()):
    rows, model = normed.shape
    width = weights.shape[1]
    block = KEY_VALUE_HEADS * PAIR
    return pl.pallas_call(
        ignoring(functools.partial(project_kernel, is_pair), 0, len(deps)),
        grid=(width // block,),
        in_specs=anywhere(deps)
        + [
            pl.BlockSpec((rows, model), lambda i: (0, 0)),
            pl.BlockSpec((model, block), lambda i: (0, i)),
            pl.BlockSpec((rows, PAIR), lambda i: (0, 0)),
            pl.BlockSpec((rows, PAIR), lambda i: (0, 0)),
        ],
        out_specs=pl.BlockSpec((rows, block), lambda i: (0, i)),
        out_shape=jax.ShapeDtypeStruct((rows, width), bf16),
        compiler_params=pltpu.CompilerParams(vmem_limit_bytes=16 << 20),
        cost_estimate=takes(3),
        name="project",
    )(*deps, normed, weights, cos, sin)


def unrotate_kernel(x_ref, cos_ref, sin_ref, out_ref):
    lane = lax.broadcasted_iota(jnp.int32, cos_ref.shape, 1)
    cos = jnp.where(lane >= HEAD_SIZE, 1.0, cos_ref[...])
    sin = jnp.where(lane >= HEAD_SIZE, 0.0, sin_ref[...])
    for at in range(0, x_ref.shape[1], PAIR):
        part = x_ref[:, at : at + PAIR].astype(f32)
        out_ref[:, at : at + PAIR] = (part * cos - swap_halves(part) * sin).astype(bf16)


def unrotate(x, cos, sin, deps=()):
    whole = lambda v: pl.BlockSpec(v.shape, lambda i: (0, 0))
    return pl.pallas_call(
        ignoring(unrotate_kernel, 0, len(deps)),
        grid=(1,),
        in_specs=anywhere(deps) + [whole(x), whole(cos), whole(sin)],
        out_specs=whole(x),
        out_shape=jax.ShapeDtypeStruct(x.shape, bf16),
        cost_estimate=takes(3),
        name="unrotate",
    )(*deps, x, cos, sin)


def copy_kernel(core_ref, x_ref, out_ref):
    out_ref[...] = x_ref[...]


def core_rows(core, x, deps=()):
    rows, width = x.shape
    return pl.pallas_call(
        ignoring(copy_kernel, 1, len(deps)),
        grid_spec=pltpu.PrefetchScalarGridSpec(
            num_scalar_prefetch=1,
            grid=(1,),
            in_specs=anywhere(deps) + [pl.BlockSpec((rows // 2, width), lambda i, core: (core[0], 0))],
            out_specs=pl.BlockSpec((rows // 2, width), lambda i, core: (0, 0)),
        ),
        out_shape=jax.ShapeDtypeStruct((rows // 2, width), x.dtype),
        cost_estimate=takes(1),
        name="core_rows",
    )(core, *deps, x)


def block_row(block, blocks, half):
    device = jnp.minimum(block, blocks - 1 - block)
    return pl.multiple_of(device * (2 * half) + (block % 2) * half, half)


def two_blocks(ref, step, blocks, half):
    first = ref[pl.ds(block_row(2 * step, blocks, half), half), :]
    second = ref[pl.ds(block_row(2 * step + 1, blocks, half), half), :]
    return jnp.concatenate([first, second], 0)


def one_head(ref, rows, head, low):
    part = ref[rows, (head // 2) * PAIR : (head // 2 + 1) * PAIR].astype(f32)
    lane = lax.broadcasted_iota(jnp.int32, part.shape, 1)
    if (head % 2 == 0) != low:
        part = pltpu.roll(part, HEAD_SIZE, 1)
    keep = lane < HEAD_SIZE if low else lane >= HEAD_SIZE
    return jnp.where(keep, part, 0.0).astype(bf16)


def allowed_keys(step, block, length, half):
    shape = (2 * half, half)
    key_pos = lax.broadcasted_iota(jnp.int32, shape, 0) + step * (2 * half)
    query_pos = lax.broadcasted_iota(jnp.int32, shape, 1) + block * half
    return key_pos <= jnp.minimum(query_pos, length - 1)


def key_steps(block, length, half):
    keys = jnp.minimum((block + 1) * half, length)
    return (keys + 2 * half - 1) // (2 * half)


LAST = (((1,), (1,)), ((), ()))


def ignoring(kernel, scalars, count):
    def body(*refs):
        return kernel(*refs[:scalars], *refs[scalars + count :])

    return body


def anywhere(deps):
    return [pl.BlockSpec(memory_space=pl.ANY)] * len(deps)


def takes(microseconds):
    return pl.CostEstimate(
        flops=int(microseconds * 0.45e9 * 1.1535), bytes_accessed=0, transcendentals=0
    )


def copy_all_kernel(x_ref, out_ref):
    out_ref[...] = x_ref[...]


def copy_later(x, deps):
    whole = pl.BlockSpec(x.shape, lambda i: (0, 0))
    return pl.pallas_call(
        ignoring(copy_all_kernel, 0, len(deps)),
        grid=(1,),
        in_specs=anywhere(deps) + [whole],
        out_specs=whole,
        out_shape=jax.ShapeDtypeStruct(x.shape, x.dtype),
        cost_estimate=takes(1),
        name="copy_later",
    )(*deps, x)


def nothing_kernel(*refs):
    pass


def gate(values, *deps):
    values = tuple(values)
    count = len(deps)
    return pl.pallas_call(
        nothing_kernel,
        in_specs=anywhere(deps) + anywhere(values),
        out_specs=anywhere(values),
        out_shape=[jax.ShapeDtypeStruct(v.shape, v.dtype) for v in values],
        input_output_aliases={count + i: i for i in range(len(values))},
        cost_estimate=takes(0),
        name="gate",
    )(*deps, *values)


def forward_kernel(blocks, info_ref, q_ref, kv_ref, o_ref, lse_ref, q_sc, m_sc, l_sc, acc_sc):
    half = q_ref.shape[0] // 2
    wide = GROUP * half
    length = info_ref[0]
    scale = SCORE_SCALE * LOG2E
    for slot in range(2):
        block = info_ref[1 + slot]
        rows = slice(slot * half, (slot + 1) * half)
        for head in range(GROUP):
            q_sc[:, head * half : (head + 1) * half] = one_head(q_ref, rows, head, True).T
        m_sc[...] = jnp.full_like(m_sc, NEGATIVE)
        l_sc[...] = jnp.zeros_like(l_sc)
        acc_sc[...] = jnp.zeros_like(acc_sc)

        def work(step, masked):
            pair = two_blocks(kv_ref, step, blocks, half)
            values_t = pair.T[HEAD_SIZE:]
            if masked:
                allowed = allowed_keys(step, block, length, half)
                allowed = jnp.concatenate([allowed, allowed], 1)
            sides = [slice(i * wide // 2, (i + 1) * wide // 2) for i in range(2)]
            both = [jnp.dot(pair, q_sc[:, at], preferred_element_type=f32) for at in sides]
            for at, scores in zip(sides, both):
                if masked:
                    scores = jnp.where(allowed, scores, NEGATIVE)
                m_old = m_sc[:1, at]
                m_new = jnp.maximum(m_old, jnp.max(scores, 0, keepdims=True) * scale)
                weights = jnp.exp2(scores * scale - m_new)
                fading = jnp.exp2(m_old - m_new)
                m_sc[:1, at] = m_new
                sums = jnp.sum(weights.reshape(2 * half // 8, 8, wide // 2), 0)
                l_sc[:, at] = l_sc[:, at] * fading + sums
                acc_sc[:, at] = acc_sc[:, at] * fading + jnp.dot(
                    values_t, weights.astype(bf16), preferred_element_type=f32
                )

        steps = key_steps(block, length, half)

        @pl.loop(0, steps - 1)
        def _(step):
            work(step, False)

        work(steps - 1, True)
        total = jnp.sum(l_sc[...], 0, keepdims=True)
        result = acc_sc[...] / total
        lse = m_sc[:1] + jnp.log2(total)
        for at in range(0, GROUP, 2):
            two = [result[:, head * half : (head + 1) * half] for head in (at, at + 1)]
            o_ref[rows, at * HEAD_SIZE : (at + 2) * HEAD_SIZE] = (
                jnp.concatenate(two, 0).T.astype(bf16)
            )
        for head in range(GROUP):
            lse_ref[0, head : head + 1, rows] = lse[:, head * half : (head + 1) * half]


def attend(head, count, grown, q, pairs, info, deps=()):
    rows, keys = q.shape[0], pairs.shape[0]
    half = rows // 2
    wide = GROUP * half
    width = GROUP * HEAD_SIZE
    aliases = {1 + i: i for i in range(len(grown))}
    deps = tuple(grown) + tuple(deps)
    return pl.pallas_call(
        ignoring(functools.partial(forward_kernel, keys // half), 1, len(deps)),
        grid_spec=pltpu.PrefetchScalarGridSpec(
            num_scalar_prefetch=1,
            grid=(count,),
            in_specs=anywhere(deps)
            + [
                pl.BlockSpec((rows, width), lambda g, info: (0, head + g)),
                pl.BlockSpec((keys, PAIR), lambda g, info: (0, head + g)),
            ],
            out_specs=[
                pl.BlockSpec((rows, width), lambda g, info: (0, head + g)),
                pl.BlockSpec((1, GROUP, rows), lambda g, info: (head + g, 0, 0)),
            ],
            scratch_shapes=[
                pltpu.VMEM((PAIR, wide), bf16),
                pltpu.VMEM((8, wide), f32),
                pltpu.VMEM((8, wide), f32),
                pltpu.VMEM((HEAD_SIZE, wide), f32),
            ],
        ),
        out_shape=[
            jax.ShapeDtypeStruct(q.shape, bf16),
            jax.ShapeDtypeStruct((KEY_VALUE_HEADS, GROUP, rows), f32),
        ],
        input_output_aliases=aliases,
        compiler_params=pltpu.CompilerParams(vmem_limit_bytes=20 << 20),
        cost_estimate=takes(10 * count),
        name="attend",
    )(info, *deps, q, pltpu.with_memory_space_constraint(pairs, pltpu.HBM))


def backward_kernel(
    blocks, info_ref, q_ref, do_ref, o_ref, lse_ref, kv_ref, cos_ref, sin_ref,
    dq_ref, same_ref, other_ref, both_sc, q_sc, do_sc, row_sc, dq_sc, dkv_sc, terms_sc,
):
    half = q_ref.shape[0] // 2
    wide = GROUP * half
    length = info_ref[0]
    dkv_sc[...] = jnp.zeros_like(dkv_sc)
    for slot in range(2):
        block = info_ref[1 + slot]
        rows = slice(slot * half, (slot + 1) * half)
        for head in range(GROUP):
            at = slice(head * half, (head + 1) * half)
            query = one_head(q_ref, rows, head, True)
            grad = one_head(do_ref, rows, head, False)
            both_sc[head * half : (head + 1) * half] = query
            both_sc[wide + head * half : wide + (head + 1) * half] = grad
            q_sc[:, at] = query.T
            do_sc[:, at] = grad.T
            row_sc[1:2, at] = lse_ref[0, head : head + 1, rows]
        for at in range(0, GROUP, 2):
            lanes = slice(at * HEAD_SIZE, (at + 2) * HEAD_SIZE)
            product = (do_ref[rows, lanes].astype(f32) * o_ref[rows, lanes].astype(f32)).T
            for i in range(2):
                row_sc[:1, (at + i) * half : (at + i + 1) * half] = jnp.sum(
                    product[i * HEAD_SIZE : (i + 1) * HEAD_SIZE], 0, keepdims=True
                )
        dq_sc[...] = jnp.zeros_like(dq_sc)

        def work(step, masked):
            pair = two_blocks(kv_ref, step, blocks, half)
            keys_t = pair.T[:HEAD_SIZE]
            if masked:
                allowed = allowed_keys(step, block, length, half)
            sides = [slice(head * half, (head + 1) * half) for head in range(GROUP)]

            def products(at):
                return (
                    jnp.dot(pair, q_sc[:, at], preferred_element_type=f32),
                    jnp.dot(pair, do_sc[:, at], preferred_element_type=f32),
                )

            coming = products(sides[0])
            for head, at in enumerate(sides):
                scores, grad_probs = coming
                if head + 1 < GROUP:
                    coming = products(sides[head + 1])
                probs = jnp.exp2(scores * (SCORE_SCALE * LOG2E) - row_sc[1:2, at])
                if masked:
                    probs = jnp.where(allowed, probs, 0.0)
                grad_scores = (probs * (grad_probs - row_sc[:1, at])).astype(bf16)
                terms_sc[:, at] = grad_scores
                terms_sc[:, wide + head * half : wide + (head + 1) * half] = probs.astype(bf16)
                dq_sc[:, at] += jnp.dot(keys_t, grad_scores, preferred_element_type=f32)
            update = jnp.dot(terms_sc[...], both_sc[...], preferred_element_type=f32)
            for i in range(2):
                at = pl.ds(block_row(2 * step + i, blocks, half), half)
                dkv_sc[at, :] += update[i * half : (i + 1) * half]

        steps = key_steps(block, length, half)

        @pl.loop(0, steps - 1)
        def _(step):
            work(step, False)

        work(steps - 1, True)
        for at in range(0, GROUP, 2):
            two = [dq_sc[:, head * half : (head + 1) * half] for head in (at, at + 1)]
            grad = jnp.concatenate(two, 0).T * SCORE_SCALE
            grad = grad * cos_ref[rows, :] - swap_halves(grad) * sin_ref[rows, :]
            dq_ref[rows, at * HEAD_SIZE : (at + 2) * HEAD_SIZE] = grad.astype(bf16)
    lane = lax.broadcasted_iota(jnp.int32, (2 * half, PAIR), 1)
    scale = jnp.where(lane < HEAD_SIZE, SCORE_SCALE, 1.0)
    core = info_ref[3]
    for i in range(blocks // 4):
        rows = slice(i * 2 * half, (i + 1) * 2 * half)
        for ref, side in ((same_ref, core), (other_ref, 1 - core)):
            at = pl.ds(pl.multiple_of((2 * i + side) * 2 * half, 2 * half), 2 * half)
            ref[rows, :] = (dkv_sc[at, :] * scale).astype(bf16)


def attend_back(head, span, grown, q, grad, attended, lse, pairs, cos, sin, info, deps=()):
    rows, keys = q.shape[0], pairs.shape[0]
    half = rows // 2
    wide = GROUP * half
    width = GROUP * HEAD_SIZE
    filled = [at for at, value in enumerate(grown) if value is not None]
    aliases = {1 + i: at for i, at in enumerate(filled)}
    deps = tuple(grown[at] for at in filled) + tuple(deps)
    head_block = pl.BlockSpec((rows, width), lambda g, info: (0, head))
    half_block = pl.BlockSpec((keys // 2, PAIR), lambda g, info: (0, head - span[0]))
    table = pl.BlockSpec((rows, PAIR), lambda g, info: (0, 0))
    half_shape = pltpu.HBM((keys // 2, span[1] * PAIR), bf16)
    return pl.pallas_call(
        ignoring(functools.partial(backward_kernel, keys // half), 1, len(deps)),
        grid_spec=pltpu.PrefetchScalarGridSpec(
            num_scalar_prefetch=1,
            grid=(1,),
            in_specs=anywhere(deps)
            + [
                head_block,
                head_block,
                head_block,
                pl.BlockSpec((1, GROUP, rows), lambda g, info: (head, 0, 0)),
                pl.BlockSpec((keys, PAIR), lambda g, info: (0, head)),
                table,
                table,
            ],
            out_specs=[head_block, half_block, half_block],
            scratch_shapes=[
                pltpu.VMEM((2 * wide, PAIR), bf16),
                pltpu.VMEM((PAIR, wide), bf16),
                pltpu.VMEM((PAIR, wide), bf16),
                pltpu.VMEM((8, wide), f32),
                pltpu.VMEM((HEAD_SIZE, wide), f32),
                pltpu.VMEM((keys, PAIR), f32),
                pltpu.VMEM((2 * half, 2 * wide), bf16),
            ],
        ),
        out_shape=[pltpu.HBM(q.shape, bf16), half_shape, half_shape],
        input_output_aliases=aliases,
        compiler_params=pltpu.CompilerParams(vmem_limit_bytes=24 << 20),
        cost_estimate=takes(16),
        name="attend_back",
    )(info, *deps, q, grad, attended, lse, pltpu.with_memory_space_constraint(pairs, pltpu.HBM), cos, sin)


def outer_kernel(parts, core_ref, a_ref, b_ref, keep_ref, send_ref, at_sc):
    @pl.when(pl.program_id(0) == 0)
    def _():
        at_sc[...] = a_ref[...].T

    rows = at_sc.shape[0] // parts // 2
    for i in range(parts):
        for side, ref in enumerate((keep_ref, send_ref)):
            half = jnp.bitwise_xor(core_ref[0], side)
            start = pl.multiple_of((2 * i + half) * rows, 16)
            ref[i] = jnp.dot(
                at_sc[pl.ds(start, rows), :], b_ref[...], preferred_element_type=f32
            ).astype(bf16)


def outer_rows(core, a, b, parts, deps=()):
    tokens, model = a.shape
    width = b.shape[1]
    block = KEY_VALUE_HEADS * PAIR
    rows = model // parts // 2
    out = jax.ShapeDtypeStruct((parts, rows, width), bf16)
    spec = pl.BlockSpec((parts, rows, block), lambda i, core: (0, 0, i))
    return pl.pallas_call(
        ignoring(functools.partial(outer_kernel, parts), 1, len(deps)),
        grid_spec=pltpu.PrefetchScalarGridSpec(
            num_scalar_prefetch=1,
            grid=(width // block,),
            in_specs=anywhere(deps)
            + [
                pl.BlockSpec((tokens, model), lambda i, core: (0, 0)),
                pl.BlockSpec((tokens, block), lambda i, core: (0, i)),
            ],
            out_specs=[spec, spec],
            scratch_shapes=[pltpu.VMEM((model, tokens), bf16)],
        ),
        out_shape=[out, out],
        compiler_params=pltpu.CompilerParams(vmem_limit_bytes=20 << 20),
        cost_estimate=takes(3),
        name="outer_rows",
    )(core, *deps, a, b)


def place_kernel(count, spots_ref, *refs):
    out_ref, sems = refs[count], refs[count + 1]
    copies = []
    for i, ref in enumerate(refs[:count]):
        start = pl.multiple_of(spots_ref[i], 16)
        copy = pltpu.make_async_copy(ref, out_ref.at[pl.ds(start, ref.shape[0])], sems.at[i])
        copy.start()
        copies.append(copy)
    for copy in copies:
        copy.wait()


def place(pieces, spots, rows):
    count = len(pieces)
    width = pieces[0].shape[1]
    return pl.pallas_call(
        functools.partial(place_kernel, count),
        grid_spec=pltpu.PrefetchScalarGridSpec(
            num_scalar_prefetch=1,
            grid=(1,),
            in_specs=anywhere(pieces),
            out_specs=pl.BlockSpec((rows, width), lambda i, spots: (0, 0)),
            scratch_shapes=[pltpu.SemaphoreType.DMA((count,))],
        ),
        out_shape=jax.ShapeDtypeStruct((rows, width), pieces[0].dtype),
        compiler_params=pltpu.CompilerParams(vmem_limit_bytes=24 << 20),
        cost_estimate=takes(3),
        name="place",
    )(jnp.stack(spots).astype(jnp.int32), *pieces)


def split_kernel(parts, core_ref, gate_ref, up_ref, out_ref):
    width = gate_ref.shape[1] // parts // 2
    for core in range(2):

        @pl.when(core_ref[0] == core)
        def _():
            taken = []
            for ref in (gate_ref, up_ref):
                for i in range(parts):
                    at = (2 * i + core) * width
                    taken.append(ref[:, at : at + width])
            out_ref[...] = jnp.concatenate(taken, 1)


def split_columns(core, gate, up, parts, deps=()):
    rows, width = gate.shape
    block = rows // 2
    spec = pl.BlockSpec((block, width), lambda i, core: (i, 0))
    return pl.pallas_call(
        ignoring(functools.partial(split_kernel, parts), 1, len(deps)),
        grid_spec=pltpu.PrefetchScalarGridSpec(
            num_scalar_prefetch=1,
            grid=(2,),
            in_specs=anywhere(deps) + [spec, spec],
            out_specs=spec,
        ),
        out_shape=jax.ShapeDtypeStruct((rows, width), gate.dtype),
        cost_estimate=takes(3.5),
        name="split_columns",
    )(core, *deps, gate, up)


def merge_kernel(parts, core_ref, own_ref, other_ref, out_ref):
    width = own_ref.shape[1] // parts
    for core in range(2):

        @pl.when(core_ref[0] == core)
        def _():
            taken = []
            for i in range(parts):
                for ref in (own_ref, other_ref) if core == 0 else (other_ref, own_ref):
                    taken.append(ref[:, i * width : (i + 1) * width].astype(f32))
            out_ref[...] = jnp.concatenate(taken, 1)


def merge_columns(core, own, other, parts):
    rows, width = own.shape
    block = rows // 4 if rows % 64 == 0 else rows // 2
    spec = pl.BlockSpec((block, width), lambda i, core: (i, 0))
    return pl.pallas_call(
        functools.partial(merge_kernel, parts),
        grid_spec=pltpu.PrefetchScalarGridSpec(
            num_scalar_prefetch=1,
            grid=(rows // block,),
            in_specs=[spec, spec],
            out_specs=pl.BlockSpec((block, 2 * width), lambda i, core: (i, 0)),
        ),
        out_shape=jax.ShapeDtypeStruct((rows, 2 * width), f32),
        compiler_params=pltpu.CompilerParams(vmem_limit_bytes=24 << 20),
        cost_estimate=takes(2.7),
        name="merge_columns",
    )(core, own, other)


def after(value, *others):
    return lax.optimization_barrier((value,) + others)[0]


class Moves:
    def __init__(self):
        self.ctx, self.fsdp = lax.axis_size("ctx"), lax.axis_size("fsdp")
        self.me, self.where = lax.axis_index("fsdp"), lax.axis_index("ctx")
        self.core = self.where % 2
        self.square = self.fsdp == 4
        self.line = self.ctx == 8

    def across(self, value, bit):
        return lax.ppermute(value, "fsdp", [(i, i ^ bit) for i in range(self.fsdp)])

    def swap(self, value):
        return lax.ppermute(value, "ctx", [(i, i ^ 1) for i in range(self.ctx)])

    def pick(self, low, high):
        return jnp.where(self.core == 0, low, high)

    def owner(self, half):
        return half if half < self.ctx else 2 * self.ctx - 1 - half

    def balance(self, rows):
        half = rows.shape[0] // 2
        return jnp.concatenate(
            [
                lax.ppermute(
                    rows[i * half : (i + 1) * half],
                    "ctx",
                    [(d, self.owner(2 * d + i)) for d in range(self.ctx)],
                )
                for i in range(2)
            ],
            0,
        )

    def restore(self, rows):
        half = rows.shape[0] // 2
        return jnp.concatenate(
            [
                lax.ppermute(
                    rows[i * half : (i + 1) * half],
                    "ctx",
                    [(self.owner(2 * d + i), d) for d in range(self.ctx)],
                )
                for i in range(2)
            ],
            0,
        )

    def gather_all(self, own):
        return lax.all_gather(own, "fsdp", axis=0, tiled=True)

    def gather_first(self, own):
        return (self.across(own, 1), self.across(own, 2)) if self.square else ()

    def gather_last(self, own, arrived, hold=None):
        if not self.square:
            return self.gather_all(own)
        rows = own.shape[0]
        half = rows // 32 * 16
        by_x, by_y = arrived
        top, bottom = self.across(by_x[:half], 2), self.across(by_y[half:], 1)
        if hold is not None:
            top, bottom = gate((top, bottom), hold)
        me = self.me
        spots = [me * rows, (me ^ 1) * rows, (me ^ 2) * rows, (me ^ 3) * rows, (me ^ 3) * rows + half]
        return place([own, by_x, by_y, top, bottom], spots, 4 * rows)

    def chip(self, value, bit):
        return lax.ppermute(value, "ctx", [(i, i ^ (2 * bit)) for i in range(self.ctx)])

    def gather_pairs(self, pairs):
        if not self.line:
            return lax.all_gather(pairs, "ctx", axis=0, tiled=True)
        rows = pairs.shape[0]
        pieces, spots = [], []
        for bit in (0, 3, 2, 1):
            piece = pairs if bit == 0 else self.chip(pairs, bit)
            pieces += [piece, self.swap(piece)]
            spots += [(self.where ^ (2 * bit)) * rows, (self.where ^ (2 * bit + 1)) * rows]
        return place(pieces, spots, self.ctx * rows)

    def scatter_pairs(self, kept):
        groups = [list(range(c, self.ctx, 2)) for c in range(2)]
        return lax.psum_scatter(
            kept, "ctx", scatter_dimension=0, axis_index_groups=groups, tiled=True
        )

    def scatter_at_once(self, whole):
        if not self.square:
            rows = whole.shape[1]
            flat = whole.reshape(self.fsdp * rows, -1)
            return lax.psum_scatter(flat, "fsdp", scatter_dimension=0, tiled=True), ()
        part = lambda bit: lax.dynamic_index_in_dim(whole, self.me ^ bit, 0, keepdims=False)
        moved = [self.across(part(bit), bit) for bit in (3, 1, 2)]
        wide = [value.astype(f32) for value in moved]
        total = (part(0).astype(f32) + wide[0]) + (wide[1] + wide[2])
        return total.astype(bf16), tuple(moved)

    def total_at_once(self, part):
        if not self.line:
            return self.over_line(part)
        moved = [part] + [self.chip(part, bit) for bit in (1, 2, 3)]
        z = self.where // 2
        low = lambda a, b: jnp.where(z % 2 == 0, a, b).astype(f32)
        near = low(moved[0], moved[1]) + low(moved[1], moved[0])
        far = low(moved[2], moved[3]) + low(moved[3], moved[2])
        first = jnp.where(z // 2 == 0, near, far)
        second = jnp.where(z // 2 == 0, far, near)
        return (first + second).astype(bf16)

    def over_line(self, part):
        groups = [list(range(c, self.ctx, 2)) for c in range(2)]
        return lax.psum(part, "ctx", axis_index_groups=groups)

    def along(self, value, pairs):
        return lax.ppermute(
            value, "ctx", [(2 * a + c, 2 * b + c) for a, b in pairs for c in range(2)]
        )

    def inward(self, part):
        return (self.along(part, [(0, 1), (3, 2)]),) if self.line else ()

    def crossing(self, part, arrived):
        if not self.line:
            return part, ()
        inner = part + arrived[0]
        return inner, (self.along(inner, [(1, 2), (2, 1)]),)

    def outward(self, inner, arrived):
        if not self.line:
            return inner, ()
        summed = inner + arrived[0]
        return summed, (self.along(summed, [(1, 0), (2, 3)]),)

    def settled(self, summed, arrived):
        if not self.line:
            return self.over_line(summed)
        z = self.where // 2
        return jnp.where((z == 0) | (z == 3), arrived[0], summed)

    def both_cores(self, part):
        other = self.swap(part)
        return self.pick(part, other), self.pick(other, part)


def local(
    tokens,
    lengths,
    cotangent,
    gain_one,
    query_weight,
    key_matrix,
    value_matrix,
    out_weight,
    gain_two,
    gate_weight,
    up_weight,
    down_weight,
):
    slots, block_length, model = tokens.shape
    moves = Moves()
    fsdp = moves.fsdp
    half = block_length // 2
    shard = model // fsdp
    attention_width = QUERY_HEADS * HEAD_SIZE
    pair_width = KEY_VALUE_HEADS * PAIR
    length = lengths[0]

    ctx = moves.where
    last = 2 * moves.ctx - 1
    block_a = jnp.where(ctx % 2 == 0, ctx, last - ctx).astype(jnp.int32)
    block_b = last - block_a
    info = jnp.stack([length, block_a, block_b, moves.core]).astype(jnp.int32)
    within = jnp.arange(half, dtype=jnp.int32)
    position = jnp.concatenate([block_a * half + within, block_b * half + within])
    exponent = jnp.arange(HALF_HEAD).astype(f32) * (2.0 / HEAD_SIZE)
    phase = position.astype(f32)[:, None] * jnp.power(10000.0, -exponent)[None, :]
    cos, sin = jnp.cos(phase), jnp.sin(phase)
    cos = jnp.concatenate([cos, cos, cos, cos], -1)
    sin = jnp.concatenate([-sin, sin, -sin, sin], -1)
    valid = (position < length).astype(f32)[:, None]

    core = moves.core.astype(jnp.int32)[None]
    in_half = shard // 2
    by_head = lambda w: w.reshape(shard, KEY_VALUE_HEADS, HEAD_SIZE)
    pair_weight = jnp.concatenate([by_head(key_matrix), by_head(value_matrix)], -1)
    pair_weight = pair_weight.reshape(shard, pair_width)
    gains = jnp.concatenate([gain_one, gain_two])[None, :]
    gains = jnp.pad(gains, ((0, EXTRA - 1), (0, pair_width - 2 * shard)))
    own_pair = jnp.concatenate([moves.pick(pair_weight[:in_half], pair_weight[in_half:]), gains], 0)
    x = moves.balance(tokens.reshape(block_length, model)).astype(f32)
    arrived = moves.gather_first(own_pair)
    own_query = core_rows(core, query_weight)
    whole_query = moves.gather_all(own_query)
    whole_pair = moves.gather_last(own_pair, arrived)
    whole_pair = whole_pair.reshape(fsdp, in_half + EXTRA, pair_width)
    gain_rows = whole_pair[:, in_half, : 2 * shard].astype(f32)
    gain_first = gain_rows[:, :shard].reshape(1, model)
    gain_second = gain_rows[:, shard:].reshape(1, model)
    beside = lambda two: jnp.stack(two, 1).reshape(model, -1)
    full_pair = beside(moves.both_cores(whole_pair[:, :in_half]))
    own_wide = split_columns(core, gate_weight, up_weight, fsdp)
    wide_arrived = moves.gather_first(own_wide)

    scale_one = rms_scale(x)
    normed = (x * scale_one * gain_first).astype(bf16)
    pairs = project(True, normed, full_pair, cos, sin)
    all_pairs = lax.all_gather(pairs, "ctx", axis=0, tiled=True)
    (whole_query,) = gate((whole_query,), pairs, own_wide)
    full_query = beside(moves.both_cores(whole_query.reshape(fsdp, in_half, -1)))
    queries = project(False, normed, full_query, cos, sin)
    own_out = core_rows(core, out_weight, (queries,))
    whole_out = moves.gather_all(own_out)
    own_down = core_rows(core, down_weight, (own_out,))
    full_down = moves.gather_all(own_down)
    if wide_arrived:
        wide_arrived = gate(wide_arrived, queries)
    late = copy_later(cotangent.reshape(block_length, model), (all_pairs, queries))
    cotangent_rows = moves.balance(late)
    ff_half = gate_weight.shape[1] // fsdp // 2
    ff_core = ff_half * fsdp
    grown = attend(0, 3, (), queries, all_pairs, info, (own_down, late))
    full_wide = moves.gather_last(own_wide, wide_arrived, grown[1])
    (whole_out,) = gate((whole_out,), grown[1])
    out_cores = moves.both_cores(whole_out.reshape(fsdp, in_half, model))
    full_out = beside(out_cores)
    attended, log_total = attend(
        3, 2, grown, queries, all_pairs, info, (cotangent_rows, full_wide)
    )
    hidden = x + jnp.dot(attended, full_out, preferred_element_type=f32)
    scale_two = rms_scale(hidden)
    normed_two = (hidden * scale_two * gain_second).astype(bf16)

    grad_result = valid * cotangent_rows.astype(f32)
    grad_low = grad_result.astype(bf16)
    both_grad = jnp.concatenate([grad_low, moves.swap(grad_low)], 0)
    both_normed = jnp.concatenate([normed_two, moves.swap(normed_two)], 0)
    wide = jnp.dot(both_normed, full_wide, preferred_element_type=f32)
    gate_pre, up_pre = wide[:, :ff_core], wide[:, ff_core:]
    sigmoid = jax.nn.sigmoid(gate_pre)
    silu = gate_pre * sigmoid
    inner = (silu * up_pre).astype(bf16)
    grad_inner = lax.dot_general(both_grad, full_down, LAST, preferred_element_type=f32)
    grad_gate_pre = grad_inner * up_pre * sigmoid * (1.0 + gate_pre * (1.0 - sigmoid))
    grad_up_pre = grad_inner * silu
    grad_wide = jnp.concatenate([grad_gate_pre.astype(bf16), grad_up_pre.astype(bf16)], 1)
    first = (((0,), (0,)), ((), ()))
    outer = lambda a, b: lax.dot_general(a, b, first, preferred_element_type=f32).astype(bf16)
    partial = lax.dot_general(grad_wide, full_wide, LAST, preferred_element_type=f32)
    grad_normed_two = partial[:block_length] + moves.swap(partial[block_length:].astype(bf16))
    grad_gain_two = jnp.sum(grad_normed_two * hidden * scale_two, 0)
    grad_hidden = grad_result + norm_back(grad_normed_two, hidden, scale_two, gain_second)
    hidden_low = grad_hidden.astype(bf16)
    shared = lambda grad: lax.psum_scatter(grad, "fsdp", scatter_dimension=0, tiled=True)
    gate_terms = outer(both_normed, grad_wide[:, :ff_core])
    up_terms = outer(both_normed, grad_wide[:, ff_core:])
    gate_shared, up_shared = shared(gate_terms), shared(up_terms)

    grad_attended = lax.dot_general(
        hidden_low, full_out, LAST, preferred_element_type=f32
    ).astype(bf16)

    def back(head, span, grown, *deps):
        return attend_back(
            head, span, grown, queries, grad_attended, attended, log_total, all_pairs, cos, sin,
            info, deps,
        )

    span = (0, KEY_VALUE_HEADS)
    grown = back(0, span, (None, None, None), gate_terms, up_terms)
    (inner,) = gate((inner,), grown[0])
    partial_out = jnp.dot(inner, full_down, preferred_element_type=f32)
    grown = back(1, span, grown, partial_out)
    result = hidden + (
        partial_out[:block_length] + moves.swap(partial_out[block_length:].astype(bf16))
    )
    output = moves.restore((valid * result).astype(bf16))
    down_terms = outer(inner, both_grad)
    down_shared = shared(down_terms)
    gate_in = moves.inward(gate_shared)
    grown = back(2, span, grown, down_terms, gate_shared)
    grown = back(3, span, grown)
    gate_inner, gate_across = moves.crossing(gate_shared, gate_in)
    grown = back(4, span, grown, output, *gate_in)
    grad_query_pre, same, other = grown

    pair_sum = moves.scatter_pairs(same + moves.swap(other))
    up_shared, down_shared = gate((up_shared, down_shared), grad_query_pre)
    up_in = moves.inward(up_shared)
    down_in = moves.inward(down_shared)
    gate_sum, gate_out = moves.outward(gate_inner, gate_across)
    from_out = outer_rows(core, attended, hidden_low, fsdp, (grad_query_pre,))
    from_query = outer_rows(core, normed, grad_query_pre, fsdp)
    square = [jnp.concatenate(two, 2) for two in zip(from_out, from_query)]
    square_shared = shared((square[0] + moves.swap(square[1])).reshape(model // 2, -1))
    by_query = lax.dot_general(grad_query_pre, full_query, LAST, preferred_element_type=f32)

    up_inner, up_across = moves.crossing(up_shared, up_in)
    down_inner, down_across = moves.crossing(down_shared, down_in)
    grad_pair_pre = unrotate(pair_sum, cos, sin, (by_query,) + up_in + down_in + gate_out)
    by_pair = lax.dot_general(grad_pair_pre, full_pair, LAST, preferred_element_type=f32)
    from_pair = outer_rows(core, normed, grad_pair_pre, fsdp)
    grad_normed = by_query + by_pair
    grad_gain_one = jnp.sum(grad_normed * x * scale_one, 0)
    grad_tokens = (grad_hidden + norm_back(grad_normed, x, scale_one, gain_first)).astype(bf16)
    gain_grads = jnp.stack([grad_gain_one.reshape(fsdp, shard), grad_gain_two.reshape(fsdp, shard)], 1)
    gain_grads = jnp.pad(
        gain_grads[:, :, None].astype(bf16),
        ((0, 0), (0, 0), (0, EXTRA - 1), (0, pair_width - shard)),
    )
    mine_too = moves.pick(gain_grads[:, 0], gain_grads[:, 1])
    others_too = moves.pick(gain_grads[:, 1], gain_grads[:, 0])
    keep = jnp.concatenate([from_pair[0], mine_too], 1)
    send = jnp.concatenate([from_pair[1], others_too], 1)
    pair_shared = shared((keep + moves.swap(send)).reshape(fsdp * (in_half + EXTRA), -1))
    pair_part = moves.over_line(pair_shared)
    square_part = moves.over_line(square_shared)
    grad_tokens = moves.restore(grad_tokens)

    gate_part = moves.settled(gate_sum, gate_out)
    gate_other = moves.swap(gate_part)
    up_sum, up_out = moves.outward(up_inner, up_across)
    grad_gate = merge_columns(core, gate_part, gate_other, fsdp)
    up_part = moves.settled(up_sum, up_out)
    grad_up = merge_columns(core, up_part, moves.swap(up_part), fsdp)
    down_sum, down_out = moves.outward(down_inner, down_across)
    down_low, down_high = moves.both_cores(moves.settled(down_sum, down_out))
    pair_parts = moves.both_cores(pair_part)
    square_parts = moves.both_cores(square_part)

    below = lambda parts: jnp.concatenate(parts, 0).astype(f32)
    pair_grad = below([part[:in_half] for part in pair_parts])
    pair_grad = pair_grad.reshape(shard, KEY_VALUE_HEADS, PAIR)
    return (
        output.reshape(slots, block_length, model),
        grad_tokens.reshape(slots, block_length, model),
        pair_parts[0][in_half, :shard].astype(f32),
        below([part[:, model:] for part in square_parts]),
        pair_grad[:, :, :HEAD_SIZE].reshape(shard, -1),
        pair_grad[:, :, HEAD_SIZE:].reshape(shard, -1),
        below([part[:, :model] for part in square_parts]),
        pair_parts[1][in_half, :shard].astype(f32),
        grad_gate,
        grad_up,
        below([down_low, down_high]),
    )


def solution(mesh):
    rows, whole = P("fsdp", None), P("fsdp", "ctx", None)
    return jax.shard_map(
        local,
        mesh=mesh,
        in_specs=(
            whole, P("fsdp"), whole, P("fsdp"), rows, rows, rows, rows, P("fsdp"), rows, rows, rows,
        ),
        out_specs=(
            whole, whole, P("fsdp"), rows, rows, rows, rows, P("fsdp"), rows, rows, rows,
        ),
        check_vma=False,
    )
```

```python
import functools
import math

import jax
import jax.numpy as jnp
from jax import lax
from jax.experimental import pallas as pl
from jax.experimental.pallas import tpu as pltpu
from jax.sharding import PartitionSpec as P

QUERY_HEADS = 20
KEY_VALUE_HEADS = 5
GROUP = QUERY_HEADS // KEY_VALUE_HEADS
HEAD_SIZE = 64
PAIR = 2 * HEAD_SIZE
HALF_HEAD = HEAD_SIZE // 2
epsilon = 1e-05
LOG2E = math.log2(math.e)
SCORE_SCALE = 1.0 / math.sqrt(HEAD_SIZE)
NEGATIVE = -1e30
EXTRA = 16
f32 = jnp.float32
bf16 = jnp.bfloat16


def rms_scale(values):
    return lax.rsqrt(jnp.mean(values * values, -1, keepdims=True) + epsilon)


def norm_back(grad_normed, values, scale_rows, gain):
    weighted = grad_normed * gain
    cubed = scale_rows * scale_rows * scale_rows
    return scale_rows * weighted - values * cubed * jnp.mean(weighted * values, -1, keepdims=True)


def swap_halves(x):
    lane = lax.broadcasted_iota(jnp.int32, x.shape, 1)
    ahead = pltpu.roll(x, PAIR - HALF_HEAD, 1)
    behind = pltpu.roll(x, HALF_HEAD, 1)
    return jnp.where(lane % HEAD_SIZE < HALF_HEAD, ahead, behind)


def project_kernel(is_pair, x_ref, w_ref, cos_ref, sin_ref, out_ref):
    product = jnp.dot(x_ref[...], w_ref[...], preferred_element_type=f32)
    cos, sin = cos_ref[...], sin_ref[...]
    if is_pair:
        lane = lax.broadcasted_iota(jnp.int32, cos.shape, 1)
        cos = jnp.where(lane >= HEAD_SIZE, 1.0, cos)
        sin = jnp.where(lane >= HEAD_SIZE, 0.0, sin)
    for at in range(0, w_ref.shape[1], PAIR):
        part = product[:, at : at + PAIR]
        out_ref[:, at : at + PAIR] = (part * cos + swap_halves(part) * sin).astype(bf16)


def project(is_pair, normed, weights, cos, sin, deps=()):
    rows, model = normed.shape
    width = weights.shape[1]
    block = KEY_VALUE_HEADS * PAIR
    return pl.pallas_call(
        ignoring(functools.partial(project_kernel, is_pair), 0, len(deps)),
        grid=(width // block,),
        in_specs=anywhere(deps)
        + [
            pl.BlockSpec((rows, model), lambda i: (0, 0)),
            pl.BlockSpec((model, block), lambda i: (0, i)),
            pl.BlockSpec((rows, PAIR), lambda i: (0, 0)),
            pl.BlockSpec((rows, PAIR), lambda i: (0, 0)),
        ],
        out_specs=pl.BlockSpec((rows, block), lambda i: (0, i)),
        out_shape=jax.ShapeDtypeStruct((rows, width), bf16),
        compiler_params=pltpu.CompilerParams(vmem_limit_bytes=16 << 20),
        cost_estimate=takes(3),
        name="project",
    )(*deps, normed, weights, cos, sin)


def unrotate_kernel(x_ref, cos_ref, sin_ref, out_ref):
    lane = lax.broadcasted_iota(jnp.int32, cos_ref.shape, 1)
    cos = jnp.where(lane >= HEAD_SIZE, 1.0, cos_ref[...])
    sin = jnp.where(lane >= HEAD_SIZE, 0.0, sin_ref[...])
    for at in range(0, x_ref.shape[1], PAIR):
        part = x_ref[:, at : at + PAIR].astype(f32)
        out_ref[:, at : at + PAIR] = (part * cos - swap_halves(part) * sin).astype(bf16)


def unrotate(x, cos, sin, deps=()):
    whole = lambda v: pl.BlockSpec(v.shape, lambda i: (0, 0))
    return pl.pallas_call(
        ignoring(unrotate_kernel, 0, len(deps)),
        grid=(1,),
        in_specs=anywhere(deps) + [whole(x), whole(cos), whole(sin)],
        out_specs=whole(x),
        out_shape=jax.ShapeDtypeStruct(x.shape, bf16),
        cost_estimate=takes(3),
        name="unrotate",
    )(*deps, x, cos, sin)


def copy_kernel(core_ref, x_ref, out_ref):
    out_ref[...] = x_ref[...]


def core_rows(core, x, deps=()):
    rows, width = x.shape
    return pl.pallas_call(
        ignoring(copy_kernel, 1, len(deps)),
        grid_spec=pltpu.PrefetchScalarGridSpec(
            num_scalar_prefetch=1,
            grid=(1,),
            in_specs=anywhere(deps) + [pl.BlockSpec((rows // 2, width), lambda i, core: (core[0], 0))],
            out_specs=pl.BlockSpec((rows // 2, width), lambda i, core: (0, 0)),
        ),
        out_shape=jax.ShapeDtypeStruct((rows // 2, width), x.dtype),
        cost_estimate=takes(1),
        name="core_rows",
    )(core, *deps, x)


def block_row(block, blocks, half):
    device = jnp.minimum(block, blocks - 1 - block)
    return pl.multiple_of(device * (2 * half) + (block % 2) * half, half)


def two_blocks(ref, step, blocks, half):
    first = ref[pl.ds(block_row(2 * step, blocks, half), half), :]
    second = ref[pl.ds(block_row(2 * step + 1, blocks, half), half), :]
    return jnp.concatenate([first, second], 0)


def one_head(ref, rows, head, low):
    part = ref[rows, (head // 2) * PAIR : (head // 2 + 1) * PAIR].astype(f32)
    lane = lax.broadcasted_iota(jnp.int32, part.shape, 1)
    if (head % 2 == 0) != low:
        part = pltpu.roll(part, HEAD_SIZE, 1)
    keep = lane < HEAD_SIZE if low else lane >= HEAD_SIZE
    return jnp.where(keep, part, 0.0).astype(bf16)


def allowed_keys(step, block, length, half):
    shape = (2 * half, half)
    key_pos = lax.broadcasted_iota(jnp.int32, shape, 0) + step * (2 * half)
    query_pos = lax.broadcasted_iota(jnp.int32, shape, 1) + block * half
    return key_pos <= jnp.minimum(query_pos, length - 1)


def key_steps(block, length, half):
    keys = jnp.minimum((block + 1) * half, length)
    return (keys + 2 * half - 1) // (2 * half)


LAST = (((1,), (1,)), ((), ()))


def ignoring(kernel, scalars, count):
    def body(*refs):
        return kernel(*refs[:scalars], *refs[scalars + count :])

    return body


def anywhere(deps):
    return [pl.BlockSpec(memory_space=pl.ANY)] * len(deps)


def takes(microseconds):
    return pl.CostEstimate(
        flops=int(microseconds * 0.45e9 * 1.1535), bytes_accessed=0, transcendentals=0
    )


def copy_all_kernel(x_ref, out_ref):
    out_ref[...] = x_ref[...]


def copy_later(x, deps):
    whole = pl.BlockSpec(x.shape, lambda i: (0, 0))
    return pl.pallas_call(
        ignoring(copy_all_kernel, 0, len(deps)),
        grid=(1,),
        in_specs=anywhere(deps) + [whole],
        out_specs=whole,
        out_shape=jax.ShapeDtypeStruct(x.shape, x.dtype),
        cost_estimate=takes(1),
        name="copy_later",
    )(*deps, x)


def nothing_kernel(*refs):
    pass


def gate(values, *deps):
    values = tuple(values)
    count = len(deps)
    return pl.pallas_call(
        nothing_kernel,
        in_specs=anywhere(deps) + anywhere(values),
        out_specs=anywhere(values),
        out_shape=[jax.ShapeDtypeStruct(v.shape, v.dtype) for v in values],
        input_output_aliases={count + i: i for i in range(len(values))},
        cost_estimate=takes(0),
        name="gate",
    )(*deps, *values)


def forward_kernel(blocks, info_ref, q_ref, kv_ref, o_ref, lse_ref, q_sc, m_sc, l_sc, acc_sc):
    half = q_ref.shape[0] // 2
    wide = GROUP * half
    length = info_ref[0]
    scale = SCORE_SCALE * LOG2E
    for slot in range(2):
        block = info_ref[1 + slot]
        rows = slice(slot * half, (slot + 1) * half)
        for head in range(GROUP):
            q_sc[:, head * half : (head + 1) * half] = one_head(q_ref, rows, head, True).T
        m_sc[...] = jnp.full_like(m_sc, NEGATIVE)
        l_sc[...] = jnp.zeros_like(l_sc)
        acc_sc[...] = jnp.zeros_like(acc_sc)

        def work(step, masked):
            pair = two_blocks(kv_ref, step, blocks, half)
            values_t = pair.T[HEAD_SIZE:]
            if masked:
                allowed = allowed_keys(step, block, length, half)
                allowed = jnp.concatenate([allowed, allowed], 1)
            sides = [slice(i * wide // 2, (i + 1) * wide // 2) for i in range(2)]
            both = [jnp.dot(pair, q_sc[:, at], preferred_element_type=f32) for at in sides]
            for at, scores in zip(sides, both):
                if masked:
                    scores = jnp.where(allowed, scores, NEGATIVE)
                m_old = m_sc[:1, at]
                m_new = jnp.maximum(m_old, jnp.max(scores, 0, keepdims=True) * scale)
                weights = jnp.exp2(scores * scale - m_new)
                fading = jnp.exp2(m_old - m_new)
                m_sc[:1, at] = m_new
                sums = jnp.sum(weights.reshape(2 * half // 8, 8, wide // 2), 0)
                l_sc[:, at] = l_sc[:, at] * fading + sums
                acc_sc[:, at] = acc_sc[:, at] * fading + jnp.dot(
                    values_t, weights.astype(bf16), preferred_element_type=f32
                )

        steps = key_steps(block, length, half)

        @pl.loop(0, steps - 1)
        def _(step):
            work(step, False)

        work(steps - 1, True)
        total = jnp.sum(l_sc[...], 0, keepdims=True)
        result = acc_sc[...] / total
        lse = m_sc[:1] + jnp.log2(total)
        for at in range(0, GROUP, 2):
            two = [result[:, head * half : (head + 1) * half] for head in (at, at + 1)]
            o_ref[rows, at * HEAD_SIZE : (at + 2) * HEAD_SIZE] = (
                jnp.concatenate(two, 0).T.astype(bf16)
            )
        for head in range(GROUP):
            lse_ref[0, head : head + 1, rows] = lse[:, head * half : (head + 1) * half]


def attend(head, count, grown, q, pairs, info, deps=()):
    rows, keys = q.shape[0], pairs.shape[0]
    half = rows // 2
    wide = GROUP * half
    width = GROUP * HEAD_SIZE
    aliases = {1 + i: i for i in range(len(grown))}
    deps = tuple(grown) + tuple(deps)
    return pl.pallas_call(
        ignoring(functools.partial(forward_kernel, keys // half), 1, len(deps)),
        grid_spec=pltpu.PrefetchScalarGridSpec(
            num_scalar_prefetch=1,
            grid=(count,),
            in_specs=anywhere(deps)
            + [
                pl.BlockSpec((rows, width), lambda g, info: (0, head + g)),
                pl.BlockSpec((keys, PAIR), lambda g, info: (0, head + g)),
            ],
            out_specs=[
                pl.BlockSpec((rows, width), lambda g, info: (0, head + g)),
                pl.BlockSpec((1, GROUP, rows), lambda g, info: (head + g, 0, 0)),
            ],
            scratch_shapes=[
                pltpu.VMEM((PAIR, wide), bf16),
                pltpu.VMEM((8, wide), f32),
                pltpu.VMEM((8, wide), f32),
                pltpu.VMEM((HEAD_SIZE, wide), f32),
            ],
        ),
        out_shape=[
            jax.ShapeDtypeStruct(q.shape, bf16),
            jax.ShapeDtypeStruct((KEY_VALUE_HEADS, GROUP, rows), f32),
        ],
        input_output_aliases=aliases,
        compiler_params=pltpu.CompilerParams(vmem_limit_bytes=20 << 20),
        cost_estimate=takes(10 * count),
        name="attend",
    )(info, *deps, q, pltpu.with_memory_space_constraint(pairs, pltpu.HBM))


def backward_kernel(
    blocks, info_ref, q_ref, do_ref, o_ref, lse_ref, kv_ref, cos_ref, sin_ref,
    dq_ref, same_ref, other_ref, both_sc, q_sc, do_sc, row_sc, dq_sc, dkv_sc, terms_sc,
):
    half = q_ref.shape[0] // 2
    wide = GROUP * half
    length = info_ref[0]
    dkv_sc[...] = jnp.zeros_like(dkv_sc)
    for slot in range(2):
        block = info_ref[1 + slot]
        rows = slice(slot * half, (slot + 1) * half)
        for head in range(GROUP):
            at = slice(head * half, (head + 1) * half)
            query = one_head(q_ref, rows, head, True)
            grad = one_head(do_ref, rows, head, False)
            both_sc[head * half : (head + 1) * half] = query
            both_sc[wide + head * half : wide + (head + 1) * half] = grad
            q_sc[:, at] = query.T
            do_sc[:, at] = grad.T
            row_sc[1:2, at] = lse_ref[0, head : head + 1, rows]
        for at in range(0, GROUP, 2):
            lanes = slice(at * HEAD_SIZE, (at + 2) * HEAD_SIZE)
            product = (do_ref[rows, lanes].astype(f32) * o_ref[rows, lanes].astype(f32)).T
            for i in range(2):
                row_sc[:1, (at + i) * half : (at + i + 1) * half] = jnp.sum(
                    product[i * HEAD_SIZE : (i + 1) * HEAD_SIZE], 0, keepdims=True
                )
        dq_sc[...] = jnp.zeros_like(dq_sc)

        def work(step, masked):
            pair = two_blocks(kv_ref, step, blocks, half)
            keys_t = pair.T[:HEAD_SIZE]
            if masked:
                allowed = allowed_keys(step, block, length, half)
            sides = [slice(head * half, (head + 1) * half) for head in range(GROUP)]

            def products(at):
                return (
                    jnp.dot(pair, q_sc[:, at], preferred_element_type=f32),
                    jnp.dot(pair, do_sc[:, at], preferred_element_type=f32),
                )

            coming = products(sides[0])
            for head, at in enumerate(sides):
                scores, grad_probs = coming
                if head + 1 < GROUP:
                    coming = products(sides[head + 1])
                probs = jnp.exp2(scores * (SCORE_SCALE * LOG2E) - row_sc[1:2, at])
                if masked:
                    probs = jnp.where(allowed, probs, 0.0)
                grad_scores = (probs * (grad_probs - row_sc[:1, at])).astype(bf16)
                terms_sc[:, at] = grad_scores
                terms_sc[:, wide + head * half : wide + (head + 1) * half] = probs.astype(bf16)
                dq_sc[:, at] += jnp.dot(keys_t, grad_scores, preferred_element_type=f32)
            update = jnp.dot(terms_sc[...], both_sc[...], preferred_element_type=f32)
            for i in range(2):
                at = pl.ds(block_row(2 * step + i, blocks, half), half)
                dkv_sc[at, :] += update[i * half : (i + 1) * half]

        steps = key_steps(block, length, half)

        @pl.loop(0, steps - 1)
        def _(step):
            work(step, False)

        work(steps - 1, True)
        for at in range(0, GROUP, 2):
            two = [dq_sc[:, head * half : (head + 1) * half] for head in (at, at + 1)]
            grad = jnp.concatenate(two, 0).T * SCORE_SCALE
            grad = grad * cos_ref[rows, :] - swap_halves(grad) * sin_ref[rows, :]
            dq_ref[rows, at * HEAD_SIZE : (at + 2) * HEAD_SIZE] = grad.astype(bf16)
    lane = lax.broadcasted_iota(jnp.int32, (2 * half, PAIR), 1)
    scale = jnp.where(lane < HEAD_SIZE, SCORE_SCALE, 1.0)
    core = info_ref[3]
    for i in range(blocks // 4):
        rows = slice(i * 2 * half, (i + 1) * 2 * half)
        for ref, side in ((same_ref, core), (other_ref, 1 - core)):
            at = pl.ds(pl.multiple_of((2 * i + side) * 2 * half, 2 * half), 2 * half)
            ref[rows, :] = (dkv_sc[at, :] * scale).astype(bf16)


def attend_back(head, span, grown, q, grad, attended, lse, pairs, cos, sin, info, deps=()):
    rows, keys = q.shape[0], pairs.shape[0]
    half = rows // 2
    wide = GROUP * half
    width = GROUP * HEAD_SIZE
    filled = [at for at, value in enumerate(grown) if value is not None]
    aliases = {1 + i: at for i, at in enumerate(filled)}
    deps = tuple(grown[at] for at in filled) + tuple(deps)
    head_block = pl.BlockSpec((rows, width), lambda g, info: (0, head))
    half_block = pl.BlockSpec((keys // 2, PAIR), lambda g, info: (0, head - span[0]))
    table = pl.BlockSpec((rows, PAIR), lambda g, info: (0, 0))
    half_shape = pltpu.HBM((keys // 2, span[1] * PAIR), bf16)
    return pl.pallas_call(
        ignoring(functools.partial(backward_kernel, keys // half), 1, len(deps)),
        grid_spec=pltpu.PrefetchScalarGridSpec(
            num_scalar_prefetch=1,
            grid=(1,),
            in_specs=anywhere(deps)
            + [
                head_block,
                head_block,
                head_block,
                pl.BlockSpec((1, GROUP, rows), lambda g, info: (head, 0, 0)),
                pl.BlockSpec((keys, PAIR), lambda g, info: (0, head)),
                table,
                table,
            ],
            out_specs=[head_block, half_block, half_block],
            scratch_shapes=[
                pltpu.VMEM((2 * wide, PAIR), bf16),
                pltpu.VMEM((PAIR, wide), bf16),
                pltpu.VMEM((PAIR, wide), bf16),
                pltpu.VMEM((8, wide), f32),
                pltpu.VMEM((HEAD_SIZE, wide), f32),
                pltpu.VMEM((keys, PAIR), f32),
                pltpu.VMEM((2 * half, 2 * wide), bf16),
            ],
        ),
        out_shape=[pltpu.HBM(q.shape, bf16), half_shape, half_shape],
        input_output_aliases=aliases,
        compiler_params=pltpu.CompilerParams(vmem_limit_bytes=24 << 20),
        cost_estimate=takes(16),
        name="attend_back",
    )(info, *deps, q, grad, attended, lse, pltpu.with_memory_space_constraint(pairs, pltpu.HBM), cos, sin)


def outer_kernel(parts, core_ref, a_ref, b_ref, keep_ref, send_ref, at_sc):
    @pl.when(pl.program_id(0) == 0)
    def _():
        at_sc[...] = a_ref[...].T

    rows = at_sc.shape[0] // parts // 2
    for i in range(parts):
        for side, ref in enumerate((keep_ref, send_ref)):
            half = jnp.bitwise_xor(core_ref[0], side)
            start = pl.multiple_of((2 * i + half) * rows, 16)
            ref[i] = jnp.dot(
                at_sc[pl.ds(start, rows), :], b_ref[...], preferred_element_type=f32
            ).astype(bf16)


def outer_rows(core, a, b, parts, deps=()):
    tokens, model = a.shape
    width = b.shape[1]
    block = KEY_VALUE_HEADS * PAIR
    rows = model // parts // 2
    out = jax.ShapeDtypeStruct((parts, rows, width), bf16)
    spec = pl.BlockSpec((parts, rows, block), lambda i, core: (0, 0, i))
    return pl.pallas_call(
        ignoring(functools.partial(outer_kernel, parts), 1, len(deps)),
        grid_spec=pltpu.PrefetchScalarGridSpec(
            num_scalar_prefetch=1,
            grid=(width // block,),
            in_specs=anywhere(deps)
            + [
                pl.BlockSpec((tokens, model), lambda i, core: (0, 0)),
                pl.BlockSpec((tokens, block), lambda i, core: (0, i)),
            ],
            out_specs=[spec, spec],
            scratch_shapes=[pltpu.VMEM((model, tokens), bf16)],
        ),
        out_shape=[out, out],
        compiler_params=pltpu.CompilerParams(vmem_limit_bytes=20 << 20),
        cost_estimate=takes(3),
        name="outer_rows",
    )(core, *deps, a, b)


def place_kernel(count, spots_ref, *refs):
    out_ref, sems = refs[count], refs[count + 1]
    copies = []
    for i, ref in enumerate(refs[:count]):
        start = pl.multiple_of(spots_ref[i], 16)
        copy = pltpu.make_async_copy(ref, out_ref.at[pl.ds(start, ref.shape[0])], sems.at[i])
        copy.start()
        copies.append(copy)
    for copy in copies:
        copy.wait()


def place(pieces, spots, rows):
    count = len(pieces)
    width = pieces[0].shape[1]
    return pl.pallas_call(
        functools.partial(place_kernel, count),
        grid_spec=pltpu.PrefetchScalarGridSpec(
            num_scalar_prefetch=1,
            grid=(1,),
            in_specs=anywhere(pieces),
            out_specs=pl.BlockSpec((rows, width), lambda i, spots: (0, 0)),
            scratch_shapes=[pltpu.SemaphoreType.DMA((count,))],
        ),
        out_shape=jax.ShapeDtypeStruct((rows, width), pieces[0].dtype),
        compiler_params=pltpu.CompilerParams(vmem_limit_bytes=24 << 20),
        cost_estimate=takes(3),
        name="place",
    )(jnp.stack(spots).astype(jnp.int32), *pieces)


def split_kernel(parts, core_ref, gate_ref, up_ref, out_ref):
    width = gate_ref.shape[1] // parts // 2
    for core in range(2):

        @pl.when(core_ref[0] == core)
        def _():
            taken = []
            for ref in (gate_ref, up_ref):
                for i in range(parts):
                    at = (2 * i + core) * width
                    taken.append(ref[:, at : at + width])
            out_ref[...] = jnp.concatenate(taken, 1)


def split_columns(core, gate, up, parts, deps=()):
    rows, width = gate.shape
    block = rows // 2
    spec = pl.BlockSpec((block, width), lambda i, core: (i, 0))
    return pl.pallas_call(
        ignoring(functools.partial(split_kernel, parts), 1, len(deps)),
        grid_spec=pltpu.PrefetchScalarGridSpec(
            num_scalar_prefetch=1,
            grid=(2,),
            in_specs=anywhere(deps) + [spec, spec],
            out_specs=spec,
        ),
        out_shape=jax.ShapeDtypeStruct((rows, width), gate.dtype),
        cost_estimate=takes(3.5),
        name="split_columns",
    )(core, *deps, gate, up)


def merge_kernel(parts, core_ref, own_ref, other_ref, out_ref):
    width = own_ref.shape[1] // parts
    for core in range(2):

        @pl.when(core_ref[0] == core)
        def _():
            taken = []
            for i in range(parts):
                for ref in (own_ref, other_ref) if core == 0 else (other_ref, own_ref):
                    taken.append(ref[:, i * width : (i + 1) * width].astype(f32))
            out_ref[...] = jnp.concatenate(taken, 1)


def merge_columns(core, own, other, parts):
    rows, width = own.shape
    block = rows // 4 if rows % 64 == 0 else rows // 2
    spec = pl.BlockSpec((block, width), lambda i, core: (i, 0))
    return pl.pallas_call(
        functools.partial(merge_kernel, parts),
        grid_spec=pltpu.PrefetchScalarGridSpec(
            num_scalar_prefetch=1,
            grid=(rows // block,),
            in_specs=[spec, spec],
            out_specs=pl.BlockSpec((block, 2 * width), lambda i, core: (i, 0)),
        ),
        out_shape=jax.ShapeDtypeStruct((rows, 2 * width), f32),
        compiler_params=pltpu.CompilerParams(vmem_limit_bytes=24 << 20),
        cost_estimate=takes(2.7),
        name="merge_columns",
    )(core, own, other)


def after(value, *others):
    return lax.optimization_barrier((value,) + others)[0]


class Moves:
    def __init__(self):
        self.ctx, self.fsdp = lax.axis_size("ctx"), lax.axis_size("fsdp")
        self.me, self.where = lax.axis_index("fsdp"), lax.axis_index("ctx")
        self.core = self.where % 2
        self.square = self.fsdp == 4
        self.line = self.ctx == 8

    def across(self, value, bit):
        return lax.ppermute(value, "fsdp", [(i, i ^ bit) for i in range(self.fsdp)])

    def swap(self, value):
        return lax.ppermute(value, "ctx", [(i, i ^ 1) for i in range(self.ctx)])

    def pick(self, low, high):
        return jnp.where(self.core == 0, low, high)

    def owner(self, half):
        return half if half < self.ctx else 2 * self.ctx - 1 - half

    def balance(self, rows):
        half = rows.shape[0] // 2
        return jnp.concatenate(
            [
                lax.ppermute(
                    rows[i * half : (i + 1) * half],
                    "ctx",
                    [(d, self.owner(2 * d + i)) for d in range(self.ctx)],
                )
                for i in range(2)
            ],
            0,
        )

    def restore(self, rows):
        half = rows.shape[0] // 2
        return jnp.concatenate(
            [
                lax.ppermute(
                    rows[i * half : (i + 1) * half],
                    "ctx",
                    [(self.owner(2 * d + i), d) for d in range(self.ctx)],
                )
                for i in range(2)
            ],
            0,
        )

    def gather_all(self, own):
        return lax.all_gather(own, "fsdp", axis=0, tiled=True)

    def gather_first(self, own):
        return (self.across(own, 1), self.across(own, 2)) if self.square else ()

    def gather_last(self, own, arrived, hold=None):
        if not self.square:
            return self.gather_all(own)
        rows = own.shape[0]
        half = rows // 32 * 16
        by_x, by_y = arrived
        top, bottom = self.across(by_x[:half], 2), self.across(by_y[half:], 1)
        if hold is not None:
            top, bottom = gate((top, bottom), hold)
        me = self.me
        spots = [me * rows, (me ^ 1) * rows, (me ^ 2) * rows, (me ^ 3) * rows, (me ^ 3) * rows + half]
        return place([own, by_x, by_y, top, bottom], spots, 4 * rows)

    def chip(self, value, bit):
        return lax.ppermute(value, "ctx", [(i, i ^ (2 * bit)) for i in range(self.ctx)])

    def gather_pairs(self, pairs):
        if not self.line:
            return lax.all_gather(pairs, "ctx", axis=0, tiled=True)
        rows = pairs.shape[0]
        pieces, spots = [], []
        for bit in (0, 3, 2, 1):
            piece = pairs if bit == 0 else self.chip(pairs, bit)
            pieces += [piece, self.swap(piece)]
            spots += [(self.where ^ (2 * bit)) * rows, (self.where ^ (2 * bit + 1)) * rows]
        return place(pieces, spots, self.ctx * rows)

    def scatter_pairs(self, kept):
        groups = [list(range(c, self.ctx, 2)) for c in range(2)]
        return lax.psum_scatter(
            kept, "ctx", scatter_dimension=0, axis_index_groups=groups, tiled=True
        )

    def scatter_at_once(self, whole):
        if not self.square:
            rows = whole.shape[1]
            flat = whole.reshape(self.fsdp * rows, -1)
            return lax.psum_scatter(flat, "fsdp", scatter_dimension=0, tiled=True), ()
        part = lambda bit: lax.dynamic_index_in_dim(whole, self.me ^ bit, 0, keepdims=False)
        moved = [self.across(part(bit), bit) for bit in (3, 1, 2)]
        wide = [value.astype(f32) for value in moved]
        total = (part(0).astype(f32) + wide[0]) + (wide[1] + wide[2])
        return total.astype(bf16), tuple(moved)

    def total_at_once(self, part):
        if not self.line:
            return self.over_line(part)
        moved = [part] + [self.chip(part, bit) for bit in (1, 2, 3)]
        z = self.where // 2
        low = lambda a, b: jnp.where(z % 2 == 0, a, b).astype(f32)
        near = low(moved[0], moved[1]) + low(moved[1], moved[0])
        far = low(moved[2], moved[3]) + low(moved[3], moved[2])
        first = jnp.where(z // 2 == 0, near, far)
        second = jnp.where(z // 2 == 0, far, near)
        return (first + second).astype(bf16)

    def over_line(self, part):
        groups = [list(range(c, self.ctx, 2)) for c in range(2)]
        return lax.psum(part, "ctx", axis_index_groups=groups)

    def along(self, value, pairs):
        return lax.ppermute(
            value, "ctx", [(2 * a + c, 2 * b + c) for a, b in pairs for c in range(2)]
        )

    def inward(self, part):
        return (self.along(part, [(0, 1), (3, 2)]),) if self.line else ()

    def crossing(self, part, arrived):
        if not self.line:
            return part, ()
        inner = part + arrived[0]
        return inner, (self.along(inner, [(1, 2), (2, 1)]),)

    def outward(self, inner, arrived):
        if not self.line:
            return inner, ()
        summed = inner + arrived[0]
        return summed, (self.along(summed, [(1, 0), (2, 3)]),)

    def settled(self, summed, arrived):
        if not self.line:
            return self.over_line(summed)
        z = self.where // 2
        return jnp.where((z == 0) | (z == 3), arrived[0], summed)

    def both_cores(self, part):
        other = self.swap(part)
        return self.pick(part, other), self.pick(other, part)


def local(
    tokens,
    lengths,
    cotangent,
    gain_one,
    query_weight,
    key_matrix,
    value_matrix,
    out_weight,
    gain_two,
    gate_weight,
    up_weight,
    down_weight,
):
    slots, block_length, model = tokens.shape
    moves = Moves()
    fsdp = moves.fsdp
    half = block_length // 2
    shard = model // fsdp
    attention_width = QUERY_HEADS * HEAD_SIZE
    pair_width = KEY_VALUE_HEADS * PAIR
    length = lengths[0]

    ctx = moves.where
    last = 2 * moves.ctx - 1
    block_a = jnp.where(ctx % 2 == 0, ctx, last - ctx).astype(jnp.int32)
    block_b = last - block_a
    info = jnp.stack([length, block_a, block_b, moves.core]).astype(jnp.int32)
    within = jnp.arange(half, dtype=jnp.int32)
    position = jnp.concatenate([block_a * half + within, block_b * half + within])
    exponent = jnp.arange(HALF_HEAD).astype(f32) * (2.0 / HEAD_SIZE)
    phase = position.astype(f32)[:, None] * jnp.power(10000.0, -exponent)[None, :]
    cos, sin = jnp.cos(phase), jnp.sin(phase)
    cos = jnp.concatenate([cos, cos, cos, cos], -1)
    sin = jnp.concatenate([-sin, sin, -sin, sin], -1)
    valid = (position < length).astype(f32)[:, None]

    core = moves.core.astype(jnp.int32)[None]
    in_half = shard // 2
    by_head = lambda w: w.reshape(shard, KEY_VALUE_HEADS, HEAD_SIZE)
    pair_weight = jnp.concatenate([by_head(key_matrix), by_head(value_matrix)], -1)
    pair_weight = pair_weight.reshape(shard, pair_width)
    gains = jnp.concatenate([gain_one, gain_two])[None, :]
    gains = jnp.pad(gains, ((0, EXTRA - 1), (0, pair_width - 2 * shard)))
    own_pair = jnp.concatenate([moves.pick(pair_weight[:in_half], pair_weight[in_half:]), gains], 0)
    x = moves.balance(tokens.reshape(block_length, model)).astype(f32)
    arrived = moves.gather_first(own_pair)
    own_query = core_rows(core, query_weight)
    whole_query = moves.gather_all(own_query)
    whole_pair = moves.gather_last(own_pair, arrived)
    whole_pair = whole_pair.reshape(fsdp, in_half + EXTRA, pair_width)
    gain_rows = whole_pair[:, in_half, : 2 * shard].astype(f32)
    gain_first = gain_rows[:, :shard].reshape(1, model)
    gain_second = gain_rows[:, shard:].reshape(1, model)
    beside = lambda two: jnp.stack(two, 1).reshape(model, -1)
    full_pair = beside(moves.both_cores(whole_pair[:, :in_half]))
    own_wide = split_columns(core, gate_weight, up_weight, fsdp)
    wide_arrived = moves.gather_first(own_wide)

    scale_one = rms_scale(x)
    normed = (x * scale_one * gain_first).astype(bf16)
    pairs = project(True, normed, full_pair, cos, sin)
    all_pairs = lax.all_gather(pairs, "ctx", axis=0, tiled=True)
    (whole_query,) = gate((whole_query,), pairs, own_wide)
    full_query = beside(moves.both_cores(whole_query.reshape(fsdp, in_half, -1)))
    queries = project(False, normed, full_query, cos, sin)
    own_out = core_rows(core, out_weight, (queries,))
    whole_out = moves.gather_all(own_out)
    own_down = core_rows(core, down_weight, (own_out,))
    full_down = moves.gather_all(own_down)
    if wide_arrived:
        wide_arrived = gate(wide_arrived, queries)
    late = copy_later(cotangent.reshape(block_length, model), (all_pairs, queries))
    cotangent_rows = moves.balance(late)
    ff_half = gate_weight.shape[1] // fsdp // 2
    ff_core = ff_half * fsdp
    grown = attend(0, 3, (), queries, all_pairs, info, (late,))
    full_wide = moves.gather_last(own_wide, wide_arrived, grown[1])
    (whole_out,) = gate((whole_out,), grown[1])
    out_cores = moves.both_cores(whole_out.reshape(fsdp, in_half, model))
    full_out = beside(out_cores)
    attended, log_total = attend(
        3, 2, grown, queries, all_pairs, info, (cotangent_rows, full_wide, own_down)
    )
    hidden = x + jnp.dot(attended, full_out, preferred_element_type=f32)
    scale_two = rms_scale(hidden)
    normed_two = (hidden * scale_two * gain_second).astype(bf16)

    grad_result = valid * cotangent_rows.astype(f32)
    grad_low = grad_result.astype(bf16)
    both_grad = jnp.concatenate([grad_low, moves.swap(grad_low)], 0)
    both_normed = jnp.concatenate([normed_two, moves.swap(normed_two)], 0)
    wide = jnp.dot(both_normed, full_wide, preferred_element_type=f32)
    gate_pre, up_pre = wide[:, :ff_core], wide[:, ff_core:]
    sigmoid = jax.nn.sigmoid(gate_pre)
    silu = gate_pre * sigmoid
    inner = (silu * up_pre).astype(bf16)
    grad_inner = lax.dot_general(both_grad, full_down, LAST, preferred_element_type=f32)
    grad_gate_pre = grad_inner * up_pre * sigmoid * (1.0 + gate_pre * (1.0 - sigmoid))
    grad_up_pre = grad_inner * silu
    grad_wide = jnp.concatenate([grad_gate_pre.astype(bf16), grad_up_pre.astype(bf16)], 1)
    first = (((0,), (0,)), ((), ()))
    outer = lambda a, b: lax.dot_general(a, b, first, preferred_element_type=f32).astype(bf16)
    partial = lax.dot_general(grad_wide, full_wide, LAST, preferred_element_type=f32)
    grad_normed_two = partial[:block_length] + moves.swap(partial[block_length:].astype(bf16))
    grad_gain_two = jnp.sum(grad_normed_two * hidden * scale_two, 0)
    grad_hidden = grad_result + norm_back(grad_normed_two, hidden, scale_two, gain_second)
    hidden_low = grad_hidden.astype(bf16)
    shared = lambda grad: lax.psum_scatter(grad, "fsdp", scatter_dimension=0, tiled=True)
    gate_terms = outer(both_normed, grad_wide[:, :ff_core])
    up_terms = outer(both_normed, grad_wide[:, ff_core:])
    gate_shared, up_shared = shared(gate_terms), shared(up_terms)

    grad_attended = lax.dot_general(
        hidden_low, full_out, LAST, preferred_element_type=f32
    ).astype(bf16)

    def back(head, span, grown, *deps):
        return attend_back(
            head, span, grown, queries, grad_attended, attended, log_total, all_pairs, cos, sin,
            info, deps,
        )

    span = (0, KEY_VALUE_HEADS)
    grown = back(0, span, (None, None, None), gate_terms, up_terms)
    (inner,) = gate((inner,), grown[0])
    partial_out = jnp.dot(inner, full_down, preferred_element_type=f32)
    grown = back(1, span, grown, partial_out)
    result = hidden + (
        partial_out[:block_length] + moves.swap(partial_out[block_length:].astype(bf16))
    )
    output = moves.restore((valid * result).astype(bf16))
    down_terms = outer(inner, both_grad)
    down_shared = shared(down_terms)
    gate_in = moves.inward(gate_shared)
    grown = back(2, span, grown, down_terms, gate_shared)
    grown = back(3, span, grown)
    gate_inner, gate_across = moves.crossing(gate_shared, gate_in)
    grown = back(4, span, grown, output, *gate_in)
    grad_query_pre, same, other = grown

    pair_sum = moves.scatter_pairs(same + moves.swap(other))
    up_shared, down_shared = gate((up_shared, down_shared), grad_query_pre)
    up_in = moves.inward(up_shared)
    down_in = moves.inward(down_shared)
    gate_sum, gate_out = moves.outward(gate_inner, gate_across)
    from_out = outer_rows(core, attended, hidden_low, fsdp, (grad_query_pre,))
    from_query = outer_rows(core, normed, grad_query_pre, fsdp)
    square = [jnp.concatenate(two, 2) for two in zip(from_out, from_query)]
    square_shared = shared((square[0] + moves.swap(square[1])).reshape(model // 2, -1))
    by_query = lax.dot_general(grad_query_pre, full_query, LAST, preferred_element_type=f32)

    up_inner, up_across = moves.crossing(up_shared, up_in)
    down_inner, down_across = moves.crossing(down_shared, down_in)
    grad_pair_pre = unrotate(pair_sum, cos, sin, (by_query,) + up_in + down_in + gate_out)
    by_pair = lax.dot_general(grad_pair_pre, full_pair, LAST, preferred_element_type=f32)
    from_pair = outer_rows(core, normed, grad_pair_pre, fsdp)
    grad_normed = by_query + by_pair
    grad_gain_one = jnp.sum(grad_normed * x * scale_one, 0)
    grad_tokens = (grad_hidden + norm_back(grad_normed, x, scale_one, gain_first)).astype(bf16)
    gain_grads = jnp.stack([grad_gain_one.reshape(fsdp, shard), grad_gain_two.reshape(fsdp, shard)], 1)
    gain_grads = jnp.pad(
        gain_grads[:, :, None].astype(bf16),
        ((0, 0), (0, 0), (0, EXTRA - 1), (0, pair_width - shard)),
    )
    mine_too = moves.pick(gain_grads[:, 0], gain_grads[:, 1])
    others_too = moves.pick(gain_grads[:, 1], gain_grads[:, 0])
    keep = jnp.concatenate([from_pair[0], mine_too], 1)
    send = jnp.concatenate([from_pair[1], others_too], 1)
    pair_shared = shared((keep + moves.swap(send)).reshape(fsdp * (in_half + EXTRA), -1))
    pair_part = moves.over_line(pair_shared)
    square_part = moves.over_line(square_shared)
    grad_tokens = moves.restore(grad_tokens)

    gate_part = moves.settled(gate_sum, gate_out)
    gate_other = moves.swap(gate_part)
    up_sum, up_out = moves.outward(up_inner, up_across)
    grad_gate = merge_columns(core, gate_part, gate_other, fsdp)
    up_part = moves.settled(up_sum, up_out)
    grad_up = merge_columns(core, up_part, moves.swap(up_part), fsdp)
    down_sum, down_out = moves.outward(down_inner, down_across)
    down_low, down_high = moves.both_cores(moves.settled(down_sum, down_out))
    pair_parts = moves.both_cores(pair_part)
    square_parts = moves.both_cores(square_part)

    below = lambda parts: jnp.concatenate(parts, 0).astype(f32)
    pair_grad = below([part[:in_half] for part in pair_parts])
    pair_grad = pair_grad.reshape(shard, KEY_VALUE_HEADS, PAIR)
    return (
        output.reshape(slots, block_length, model),
        grad_tokens.reshape(slots, block_length, model),
        pair_parts[0][in_half, :shard].astype(f32),
        below([part[:, model:] for part in square_parts]),
        pair_grad[:, :, :HEAD_SIZE].reshape(shard, -1),
        pair_grad[:, :, HEAD_SIZE:].reshape(shard, -1),
        below([part[:, :model] for part in square_parts]),
        pair_parts[1][in_half, :shard].astype(f32),
        grad_gate,
        grad_up,
        below([down_low, down_high]),
    )


def solution(mesh):
    rows, whole = P("fsdp", None), P("fsdp", "ctx", None)
    return jax.shard_map(
        local,
        mesh=mesh,
        in_specs=(
            whole, P("fsdp"), whole, P("fsdp"), rows, rows, rows, rows, P("fsdp"), rows, rows, rows,
        ),
        out_specs=(
            whole, whole, P("fsdp"), rows, rows, rows, rows, P("fsdp"), rows, rows, rows,
        ),
        check_vma=False,
    )
```
